256 devices in a mesh: tm: 64 (over x, z, core), tmpl: 4 (over y).
Axes of the slice: x: 4, y: 4, z: 8, core: 2. Of those that a mesh axis runs over, the one named last changes fastest.
Arguments:
- records: float32 [4, 36864, 512], P('tmpl', 'tm'), may hold values from -6 to 6
- band_filter: float32 [65], replicated, may hold values from -0.75 to 0.75
- templates: bfloat16 [1024, 144, 128], P('tmpl'), may hold values from -6 to 6
- destinations: int32 [4, 36864], P('tmpl', 'tm'), may hold values from 0 to 63, as said below
- offsets: int32 [4, 36864], P('tmpl', 'tm'), may hold values from 0 to 294400, as said below
- live_counts: int32 [4, 64], P('tmpl', 'tm'), may hold values from 9 to 576, as said below
Outputs:
- detection: float32 [1024, 65536], P('tmpl', 'tm')
The draws below stay inside these ranges and needn't reach their ends.
Inputs may be any that keep to these rules, and one draw needn't show every extreme that they name: `destinations`: device s's 576 entries of a quarter name every window exactly 9 times, so at most 9 live records go from one device to one window; in each quarter some window has all its entries live on every device. `offsets`: multiples of 512; within a quarter every pair of destination and offset occurs exactly once over all entries of all devices. The live entries of a device are its first live_counts entries; the others are absent records.
All inputs are finite; a program needn't handle non-finite values.
Results may differ from the reference program's by a relative error of at most 0.0029.
Values may be sent and summed in bfloat16 or wider, within the bound.
A program may use at most 128 MiB of HBM per device.

```python
import jax
import jax.numpy as jnp
from jax import lax

CH = 144
TEMPLATES = 1024
TLEN = 128
RECLEN = 512
DEC = 8
TAPS = 65
SLOTS = 16
CHQ = 36
RMAX = 576
CAP = 9
RAW_WIN = 8192
WIN = 1024
LAGS = 65536
N_TM = 64
N_TMPL = 4


def routing_tables(key):
    key_ids, key_full, key_order, key_count, key_pick = jax.random.split(jax.random.fold_in(key, 7), 5)
    labels = jax.vmap(lambda sub: jax.random.permutation(sub, RMAX))(jax.random.split(key_ids, N_TMPL * N_TM))
    labels = labels.reshape(N_TMPL, N_TM, CAP, N_TM).transpose(0, 3, 1, 2).reshape(N_TMPL, N_TM, RMAX)
    entry = jnp.arange(RMAX, dtype=jnp.int32)
    window_of = entry // CAP
    full_window = jax.random.randint(key_full, (N_TMPL,), 0, N_TM)
    shuffle = jax.vmap(lambda sub: jax.random.permutation(sub, RMAX))(jax.random.split(key_order, N_TMPL * N_TM))
    shuffle = shuffle.reshape(N_TMPL, N_TM, RMAX).astype(jnp.int32)
    score = jnp.where(window_of[None, None, :] == full_window[:, None, None], shuffle - RMAX, shuffle)
    order = jnp.argsort(score, axis=-1, stable=True)
    windows = jnp.take_along_axis(jnp.broadcast_to(window_of, (N_TMPL, N_TM, RMAX)), order, -1)
    chosen = jnp.take_along_axis(labels.astype(jnp.int32), order, -1)
    counts = jax.random.randint(key_count, (N_TMPL, N_TM), CAP, RMAX + 1)
    full_sender = jax.random.randint(key_pick, (N_TMPL,), 0, N_TM)
    senders = jnp.arange(N_TM, dtype=jnp.int32)[None, :]
    counts = jnp.where(senders == full_sender[:, None], RMAX, counts)
    counts = jnp.where(senders == (full_sender[:, None] + 1) % N_TM, CAP, counts)
    return (windows.reshape(N_TMPL, N_TM * RMAX).astype(jnp.int32), (chosen * RECLEN).reshape(N_TMPL, N_TM * RMAX).astype(jnp.int32), counts.astype(jnp.int32))


def draw_destinations(key, part):
    return routing_tables(key)[0]


def draw_offsets(key, part):
    return routing_tables(key)[1]


def draw_live_counts(key, part):
    return routing_tables(key)[2]


def steps_of(key, dims, shards, smallest, top_value):
    def one(dim, parts):
        heights = jax.random.uniform(jax.random.fold_in(jax.random.fold_in(key, 6), dim), (parts,), jnp.float32, smallest / len(shards), top_value / len(shards))
        return jnp.repeat(jnp.exp(heights), dims[dim] // parts).reshape((-1,) + (1,) * (len(dims) - dim - 1))

    gain = one(*shards[0])
    for cut in shards[1:]:
        gain = gain * one(*cut)
    return gain


def scatter_about(rng, dims, scale, bound, cuts=(), kind=jnp.bfloat16):
    entries = scale * jax.random.normal(rng, dims, jnp.float32)
    if cuts:
        entries = entries * steps_of(rng, dims, cuts, -0.22, 0.18)
    return jnp.clip(entries, -bound, bound).astype(kind)


def setup_inputs(seed: int = 0) -> dict:
    splits = jax.random.split(jax.random.key(seed), 7)
    records = scatter_about(splits[0], (N_TMPL, N_TM * RMAX, RECLEN), 1.0, 6.0, ((0, 4), (1, 64)), jnp.float32)
    band_filter = scatter_about(splits[1], (TAPS,), TAPS ** -0.5, 0.75, (), jnp.float32)
    templates = scatter_about(splits[2], (TEMPLATES, CH, TLEN), 1.0, 6.0, ((0, 4),))
    destinations = draw_destinations(jax.random.fold_in(splits[6], 71), 0)
    offsets = draw_offsets(jax.random.fold_in(splits[6], 71), 0)
    live_counts = draw_live_counts(jax.random.fold_in(splits[6], 71), 0)
    return dict(records=records, band_filter=band_filter, templates=templates, destinations=destinations, offsets=offsets, live_counts=live_counts)


EPSILON = 1e-06

def place_rows(target_rows, stored):
    empty = jnp.zeros((N_TM * RMAX + 1, RECLEN), jnp.float32)
    return empty.at[target_rows].set(stored.astype(jnp.float32))

def reference(records, band_filter, templates, destinations, offsets, live_counts):
    entry = jnp.arange(N_TM * RMAX, dtype=jnp.int32) % RMAX
    sender = jnp.arange(N_TM * RMAX, dtype=jnp.int32) // RMAX
    limit = live_counts[:, sender]
    is_live = entry[None, :] < limit
    target = destinations * RMAX + offsets // RECLEN
    target = jnp.where(is_live, target, N_TM * RMAX).astype(jnp.int32)
    placed = jax.vmap(place_rows)(target, records)[:, :-1]
    stream = placed.reshape(N_TMPL, N_TM, CHQ, SLOTS, RECLEN).transpose(0, 2, 1, 3, 4).reshape(CH, N_TM * RAW_WIN)
    stream = jnp.pad(stream, ((0, 0), (0, TAPS - DEC)))
    filtered = jnp.zeros((CH, LAGS), jnp.float32)
    for tap_index in range(TAPS):
        strided = lax.slice(stream, (0, tap_index), (CH, tap_index + DEC * (LAGS - 1) + 1), (1, DEC))
        filtered = filtered + band_filter[tap_index] * strided
    decim = filtered.astype(jnp.bfloat16)
    padded = jnp.pad(decim, ((0, 0), (0, TLEN - 1)))
    wide = templates.astype(jnp.float32)
    tscale = jnp.sqrt(lax.optimization_barrier(jnp.mean(wide * wide, axis=(1, 2))) + EPSILON)
    width = min(16, TLEN)

    def one_window(window):
        piece = lax.dynamic_slice_in_dim(padded, window * WIN, WIN + TLEN - 1, 1).astype(jnp.float32)
        corr = jnp.zeros((TEMPLATES, WIN), jnp.float32)
        for group in range(TLEN // width):
            hankel = jnp.stack([piece[:, shift_at:shift_at + WIN] for shift_at in range(group * width, (group + 1) * width)], 0)
            corr = corr + jnp.einsum('kcj,jct->kt', wide[:, :, group * width:(group + 1) * width], hankel, precision=lax.Precision.HIGHEST)
        power = lax.optimization_barrier(jnp.sum(piece * piece, 0))
        running = jnp.concatenate([jnp.zeros((1,), jnp.float32), jnp.cumsum(power)])
        energy = (running[TLEN:] - running[:WIN]) / (CH * TLEN)
        return corr / (CH * TLEN * tscale[:, None] * jnp.sqrt(energy + EPSILON)[None, :])
    windows = lax.map(one_window, jnp.arange(N_TM, dtype=jnp.int32))
    return windows.transpose(1, 0, 2).reshape(TEMPLATES, LAGS)
```

```python
import jax
import jax.numpy as jnp
from jax import lax
from jax.experimental import pallas as pl
from jax.experimental.pallas import tpu as pltpu
from jax.sharding import PartitionSpec as P

CH = 144
TAPS = 65
DEC = 8
RECLEN = 512
TLEN = 128
EPSILON = 1e-06

NTM = 64
NY = 4
ENT = 576
EPAD = 640
CAP = 16
UNITS = 3
UCH = 12
KEPT = 256
WIN = 1024
F32 = jnp.float32
BF16 = jnp.bfloat16
MESH = pl.DeviceIdType.MESH
NT = (((1,), (1,)), ((), ()))


def iota(shape, dim):
    return lax.broadcasted_iota(jnp.int32, shape, dim)


def lane_take(x, index):
    return jnp.take_along_axis(x, index, axis=1)


def kernel(
    dest_ref,
    offs_ref,
    live_ref,
    band_ref,
    rec_hbm,
    tmpl_hbm,
    out_ref,
    rec,
    tmpl,
    taps,
    rows,
    ybuf,
    send,
    arr,
    wts,
    tsq,
    gall,
    g32,
    pw,
    hank,
    acc,
    rec_sem,
    tmpl_sem,
    a_send,
    a_recv,
    b_send,
    main_recv,
    halo_recv,
):
    me = lax.axis_index("tm")
    my = lax.axis_index("tmpl")

    rec_copy = pltpu.make_async_copy(rec_hbm.at[0], rec.at[pl.ds(0, ENT)], rec_sem)
    rec_copy.start()
    barrier = pltpu.get_barrier_semaphore()

    def greet(i, _):
        pl.semaphore_signal(
            barrier, inc=1, device_id={"tm": lax.rem(me + i, NTM)}, device_id_type=MESH
        )
        return 0

    lax.fori_loop(1, NTM, greet, 0)
    for i in range(1, NY):
        other = lax.rem(my + i, NY)
        pl.semaphore_signal(barrier, inc=1, device_id={"tmpl": other}, device_id_type=MESH)

        @pl.when(me < NTM - 1)
        def _():
            pl.semaphore_signal(
                barrier, inc=1, device_id={"tm": me + 1, "tmpl": other}, device_id_type=MESH
            )

    def tmpl_copy(b):
        part = pl.ds(pl.multiple_of(b * 16, 16), 16)
        return pltpu.make_async_copy(tmpl_hbm.at[part], tmpl.at[part], tmpl_sem.at[b])

    for b in range(16):
        tmpl_copy(b).start()

    rec[ENT:EPAD, :] = jnp.zeros((EPAD - ENT, RECLEN), F32)
    rows[...] = jnp.full(rows.shape, -1, jnp.int32)
    rows[0:1, 0:ENT] = dest_ref[...]
    rows[1:2, 0:ENT] = offs_ref[...]
    entry = iota((1, EPAD), 1)
    target = rows[0:1, :]
    label = jnp.maximum(rows[1:2, :], 0) // RECLEN
    chan = label // 16
    slot = label - chan * 16
    chan = chan + 4 * (chan // UCH)
    member = jnp.where(jnp.broadcast_to(target, (NTM, EPAD)) == iota((NTM, EPAD), 0), 1.0, 0.0)
    before = jnp.where(iota((EPAD, EPAD), 0) < iota((EPAD, EPAD), 1), 1.0, 0.0).astype(BF16)
    ahead = jnp.dot(member.astype(BF16), before, preferred_element_type=F32)
    rank = jnp.sum(ahead * member, axis=0, keepdims=True).astype(jnp.int32)
    live = entry < jnp.minimum(live_ref[0, 0], ENT)
    place = jnp.where(live, target * CAP + rank, -1)

    taps[...] = jnp.zeros(taps.shape, F32)
    taps[0:1, 0:TAPS] = band_ref[...]
    line = jnp.broadcast_to(taps[0:1, :], (80, 128))
    parts = []
    for s in range(4):
        tap = iota((80, 128), 1) + 128 * s + DEC * iota((80, 128), 0) - (RECLEN - DEC)
        good = (tap >= 0) & (tap < TAPS) & (iota((80, 128), 0) < 72)
        parts.append(jnp.where(good, lane_take(line, jnp.clip(tap, 0, 127)), 0.0))
    band = jnp.concatenate(parts, axis=1)
    band_hi = band.astype(BF16)
    band_lo = (band - band_hi.astype(F32)).astype(BF16)

    rec_copy.wait()
    data = rec[...]
    data_hi = data.astype(BF16)
    data_lo = (data - data_hi.astype(F32)).astype(BF16)
    parts = lax.dot_general(band_hi, data_hi, NT, preferred_element_type=F32)
    parts += lax.dot_general(band_hi, data_lo, NT, preferred_element_type=F32)
    parts += lax.dot_general(band_lo, data_hi, NT, preferred_element_type=F32)
    row = iota((80, EPAD), 0)
    parts = jnp.where(row == 72, jnp.broadcast_to(chan.astype(F32), (80, EPAD)), parts)
    parts = jnp.where(row == 73, jnp.broadcast_to(slot.astype(F32), (80, EPAD)), parts)
    parts = jnp.concatenate([parts, jnp.zeros((48, EPAD), F32)], axis=0).astype(BF16)

    ybuf[NTM * CAP :, :] = jnp.zeros((CAP, 128), F32)
    for q in range(4):
        pick = jnp.where(
            jnp.broadcast_to(place, (256, EPAD)) == iota((256, EPAD), 0) + 256 * q, 1.0, 0.0
        ).astype(BF16)
        ybuf[256 * q : 256 * q + 256, :] = lax.dot_general(
            pick, parts, NT, preferred_element_type=F32
        )
    lane = iota((256, 128), 1)
    for q in range(4):
        own = ybuf[256 * q : 256 * q + 256, :]
        after = ybuf[256 * q + CAP : 256 * q + 256 + CAP, :]
        both = jnp.where((lane >= 80) & (lane < 90), pltpu.roll(after, 16, 1), own)
        send[16 * q : 16 * q + 16] = both.astype(BF16).reshape(16, CAP, 128)

    pl.semaphore_wait(barrier, 66 + jnp.where(me > 0, 3, 0))

    def block_copy(to, frm):
        return pltpu.make_async_remote_copy(
            src_ref=send.at[to],
            dst_ref=arr.at[frm],
            send_sem=a_send,
            recv_sem=a_recv,
            device_id={"tm": to},
            device_id_type=MESH,
        )

    def send_block(i, _):
        block_copy(lax.rem(me + i, NTM), me).start()
        return 0

    lax.fori_loop(1, NTM, send_block, 0)
    arr[me] = send[me]

    def order_templates(b, _):
        tmpl_copy(b).wait()
        part = pl.ds(pl.multiple_of(b * 16, 16), 16)
        total = jnp.zeros((16, 16, 128), F32)
        for g in range(9):
            x = tmpl[part, 16 * g : 16 * g + 16, :]
            wts[16 * g : 16 * g + 16, part, :] = jnp.transpose(x, (1, 0, 2))
            wide = x.astype(F32)
            total = total + wide * wide
        tsq[part, :] = jnp.sum(total, axis=1)
        return 0

    lax.fori_loop(0, 16, order_templates, 0)

    def all_blocks():
        return pltpu.make_async_remote_copy(
            src_ref=send.at[pl.ds(0, NTM - 1)],
            dst_ref=arr.at[pl.ds(0, NTM - 1)],
            send_sem=a_send,
            recv_sem=a_recv,
            device_id={"tm": me},
            device_id_type=MESH,
        )

    all_blocks().wait_recv()

    came = arr[...].reshape(NTM * CAP, 128)
    sel_row = iota((8, 128), 0)
    sel_lane = iota((8, 128), 1)
    selector = (
        ((sel_row == 0) & (sel_lane == 72))
        | ((sel_row == 1) & (sel_lane == 73))
        | ((sel_row == 2) & (sel_lane == 88))
        | ((sel_row == 3) & (sel_lane == 89))
    )
    names = lax.dot_general(
        jnp.where(selector, 1.0, 0.0).astype(BF16), came, NT, preferred_element_type=F32
    ).astype(jnp.int32)
    spot = names[0:1, :] + 48 * (15 - names[1:2, :])
    spot_next = jnp.where(names[3:4, :] == 0, names[2:3, :], -1)
    lane = iota((48, 128), 1)
    pick = jnp.where(
        jnp.broadcast_to(spot_next, (48, 1024)) == iota((48, 1024), 0), 1.0, 0.0
    ).astype(BF16)
    carry = pltpu.roll(jnp.dot(pick, came, preferred_element_type=F32), 48, 1)
    for b in range(8):
        pick = jnp.where(
            jnp.broadcast_to(spot, (96, 1024)) == iota((96, 1024), 0) + 96 * b, 1.0, 0.0
        ).astype(BF16)
        got = jnp.dot(pick, came, preferred_element_type=F32)
        odd = pltpu.roll(got[48:96], 64, 1)
        block = (
            jnp.where(lane < 72, got[0:48], 0.0)
            + jnp.where(lane >= 64, odd, 0.0)
            + jnp.where(lane < 8, carry, 0.0)
        )
        carry = odd
        gall[my, :, :, 128 * (b + 1) : 128 * (b + 2)] = block.astype(BF16).reshape(UNITS, 16, 128)

    @pl.when(me == NTM - 1)
    def _():
        gall[:, :, :, 0:128] = jnp.zeros((NY, UNITS, 16, 128), BF16)

    def halo_copy(quarter, to_tm, to_y, k=0):
        return pltpu.make_async_remote_copy(
            src_ref=gall.at[quarter, :, :, pl.ds(WIN, 128)],
            dst_ref=gall.at[quarter, :, :, pl.ds(0, 128)],
            send_sem=b_send.at[4 + k],
            recv_sem=halo_recv.at[quarter],
            device_id={"tm": to_tm, "tmpl": to_y},
            device_id_type=MESH,
        )

    def main_copy(quarter, to_y, k=0):
        return pltpu.make_async_remote_copy(
            src_ref=gall.at[quarter, :, :, pl.ds(128, WIN)],
            dst_ref=gall.at[quarter, :, :, pl.ds(128, WIN)],
            send_sem=b_send.at[k],
            recv_sem=main_recv.at[quarter],
            device_id={"tmpl": to_y},
            device_id_type=MESH,
        )

    @pl.when(me > 0)
    def _():
        for i in (0, 1, 3, 2):
            halo_copy(my, me - 1, lax.rem(my + i, NY), i).start()

    for i in (1, 3, 2):
        main_copy(my, lax.rem(my + i, NY), i).start()

    def quarter_of(n):
        step = n // UNITS
        return lax.rem(my + lax.bitwise_xor(step, lax.shift_right_logical(step, 1)), NY)

    def arrive(n, mine):
        quarter = quarter_of(n)
        if not mine:
            main_copy(quarter, my).wait_recv()

        @pl.when(me < NTM - 1)
        def _():
            halo_copy(quarter, me, my).wait_recv()

    hl = iota((16, 128), 1)
    hr = iota((16, 128), 0)

    def build(n, side):
        wide = gall[quarter_of(n), lax.rem(n, UNITS)].astype(F32)
        g32[side] = wide
        pw[...] += wide * wide
        for i in range(UCH):
            line = [
                jnp.broadcast_to(g32[side, i : i + 1, 128 * b : 128 * b + 128], (16, 128))
                for b in range(9)
            ]
            for s in range(8):
                from_next = hl >= hr + 16 * s
                turned = [pltpu.roll(x, 16 * s, 1, stride=1, stride_axis=0) for x in line]
                for b in range(8):
                    at = i * 128 + 16 * s
                    hank[side, at : at + 16, 128 * b : 128 * b + 128] = jnp.where(
                        from_next, turned[b + 1], turned[b]
                    ).astype(BF16)

    def correlate(n, side):
        c0 = quarter_of(n) * (CH // NY) + lax.rem(n, UNITS) * UCH
        left = jnp.concatenate([wts[c0 + i] for i in range(UCH)], axis=1)
        acc[...] += jnp.dot(left, hank[side], preferred_element_type=F32)

    acc[...] = jnp.zeros(acc.shape, F32)
    pw[...] = jnp.zeros(pw.shape, F32)
    arrive(0, True)
    build(0, 0)
    total_units = NY * UNITS

    def step(it, _):
        n = 2 * it

        @pl.when((it == 1) | (it == 4))
        def _():
            arrive(n + 1, False)

        build(n + 1, 1)
        correlate(n, 0)

        @pl.when(it == 2)
        def _():
            arrive(n + 2, False)

        build(n + 2, 0)
        correlate(n + 1, 1)
        return 0

    lax.fori_loop(0, total_units // 2 - 1, step, 0)
    build(total_units - 1, 1)
    correlate(total_units - 2, 0)
    correlate(total_units - 1, 1)

    energy = jnp.broadcast_to(jnp.sum(pw[...], axis=0, keepdims=True), (8, WIN + 128))
    for k in (1, 2, 4, 8, 16, 32, 64):
        energy = energy + pltpu.roll(energy, k, 1)
    by_time = 1.0 / jnp.sqrt(energy[0:1, 128:] * (1.0 / (CH * TLEN)) + EPSILON)
    mean = jnp.sum(tsq[...], axis=1, keepdims=True) * (1.0 / (CH * TLEN))
    by_tmpl = 1.0 / (CH * TLEN * jnp.sqrt(mean + EPSILON))
    back = 127 - iota((KEPT, 128), 1)
    for b in range(8):
        part = acc[:, 128 * b : 128 * b + 128] * by_tmpl * by_time[:, 128 * b : 128 * b + 128]
        out_ref[:, 128 * (7 - b) : 128 * (8 - b)] = lane_take(part, back)

    all_blocks().wait_send()
    for i in range(1, NY):
        main_copy(my, lax.rem(my + i, NY), i).wait_send()

    @pl.when(me > 0)
    def _():
        for i in range(NY):
            halo_copy(my, me - 1, lax.rem(my + i, NY), i).wait_send()


def shards(records, band_filter, templates, destinations, offsets, live_counts):
    vmem = pl.BlockSpec(memory_space=pltpu.VMEM)
    hbm = pl.BlockSpec(memory_space=pl.ANY)
    return pl.pallas_call(
        kernel,
        out_shape=jax.ShapeDtypeStruct((KEPT, WIN), F32),
        in_specs=[vmem, vmem, pl.BlockSpec(memory_space=pltpu.SMEM), vmem, hbm, hbm],
        out_specs=vmem,
        scratch_shapes=[
            pltpu.VMEM((EPAD, RECLEN), F32),
            pltpu.VMEM((KEPT, CH, TLEN), BF16),
            pltpu.VMEM((8, 128), F32),
            pltpu.VMEM((8, EPAD), jnp.int32),
            pltpu.VMEM((NTM * CAP + CAP, 128), F32),
            pltpu.VMEM((NTM, CAP, 128), BF16),
            pltpu.VMEM((NTM, CAP, 128), BF16),
            pltpu.VMEM((CH, KEPT, TLEN), BF16),
            pltpu.VMEM((KEPT, 128), F32),
            pltpu.VMEM((NY, UNITS, 16, WIN + 128), BF16),
            pltpu.VMEM((2, 16, WIN + 128), F32),
            pltpu.VMEM((16, WIN + 128), F32),
            pltpu.VMEM((2, UCH * TLEN, WIN), BF16),
            pltpu.VMEM((KEPT, WIN), F32),
            pltpu.SemaphoreType.DMA,
            pltpu.SemaphoreType.DMA((16,)),
            pltpu.SemaphoreType.DMA,
            pltpu.SemaphoreType.DMA,
            pltpu.SemaphoreType.DMA((2 * NY,)),
            pltpu.SemaphoreType.DMA((NY,)),
            pltpu.SemaphoreType.DMA((NY,)),
        ],
        compiler_params=pltpu.CompilerParams(
            collective_id=0, has_side_effects=True, vmem_limit_bytes=56 * 1024 * 1024
        ),
    )(destinations, offsets, live_counts, band_filter.reshape(1, TAPS), records, templates)


def solution(mesh):
    in_specs = (
        P("tmpl", "tm", None),
        P(),
        P("tmpl", None, None),
        P("tmpl", "tm"),
        P("tmpl", "tm"),
        P("tmpl", "tm"),
    )
    return jax.shard_map(
        shards, mesh=mesh, in_specs=in_specs, out_specs=P("tmpl", "tm"), check_vma=False
    )
```

```python
import jax
import jax.numpy as jnp
from jax import lax
from jax.experimental import pallas as pl
from jax.experimental.pallas import tpu as pltpu
from jax.sharding import PartitionSpec as P

CH = 144
TAPS = 65
DEC = 8
RECLEN = 512
TLEN = 128
EPSILON = 1e-06

NTM = 64
NY = 4
ENT = 576
EPAD = 640
CAP = 16
WIRE = 10
UNITS = 3
UCH = 12
KEPT = 256
WIN = 1024
F32 = jnp.float32
BF16 = jnp.bfloat16
MESH = pl.DeviceIdType.MESH
FAR_FIRST = sorted(
    [(dx, dz, dc) for dx in range(4) for dz in range(8) for dc in range(2)][1:],
    key=lambda d: -(min(d[0], 4 - d[0]) + min(d[1], 8 - d[1])),
)
NT = (((1,), (1,)), ((), ()))


def iota(shape, dim):
    return lax.broadcasted_iota(jnp.int32, shape, dim)


def lane_take(x, index):
    return jnp.take_along_axis(x, index, axis=1)


def kernel(
    dest_hbm,
    offs_hbm,
    live_ref,
    band_hbm,
    rec_hbm,
    tmpl_hbm,
    acc,
    by_tmpl,
    by_time,
    rec,
    tmpl,
    taps,
    rows,
    ybuf,
    send,
    arr,
    wts,
    tsq,
    gall,
    g32,
    pw,
    hank,
    dest_ref,
    offs_ref,
    band_ref,
    rec_sem,
    tmpl_sem,
    a_send,
    a_recv,
    b_send,
    main_recv,
    halo_recv,
):
    me = lax.axis_index("tm")
    my = lax.axis_index("tmpl")

    rec_copy = pltpu.make_async_copy(rec_hbm.at[0], rec.at[pl.ds(0, ENT)], rec_sem.at[0])
    small = [
        pltpu.make_async_copy(dest_hbm, dest_ref, rec_sem.at[1]),
        pltpu.make_async_copy(offs_hbm, offs_ref, rec_sem.at[2]),
        pltpu.make_async_copy(band_hbm, band_ref, rec_sem.at[3]),
    ]
    for copy in small:
        copy.start()
    rec_copy.start()
    arr[...] = jnp.zeros(arr.shape, BF16)
    barrier = pltpu.get_barrier_semaphore()

    def greet(i, _):
        pl.semaphore_signal(
            barrier, inc=1, device_id={"tm": lax.rem(me + i, NTM)}, device_id_type=MESH
        )
        return 0

    lax.fori_loop(1, NTM, greet, 0)
    for i in range(1, NY):
        other = lax.rem(my + i, NY)
        pl.semaphore_signal(barrier, inc=1, device_id={"tmpl": other}, device_id_type=MESH)

        @pl.when(me < NTM - 1)
        def _():
            pl.semaphore_signal(
                barrier, inc=1, device_id={"tm": me + 1, "tmpl": other}, device_id_type=MESH
            )

    def tmpl_copy(b):
        part = pl.ds(pl.multiple_of(b * 16, 16), 16)
        return pltpu.make_async_copy(tmpl_hbm.at[part], tmpl.at[part], tmpl_sem.at[b])

    for b in range(16):
        tmpl_copy(b).start()

    rec[ENT:EPAD, :] = jnp.zeros((EPAD - ENT, RECLEN), F32)
    rows[...] = jnp.full(rows.shape, -1, jnp.int32)
    for copy in small:
        copy.wait()
    rows[0:1, 0:ENT] = dest_ref[...]
    rows[1:2, 0:ENT] = offs_ref[...]
    entry = iota((1, EPAD), 1)
    target = rows[0:1, :]
    label = jnp.maximum(rows[1:2, :], 0) // RECLEN
    chan = label // 16
    slot = label - chan * 16
    chan = chan + 4 * (chan // UCH)
    member = jnp.where(jnp.broadcast_to(target, (NTM, EPAD)) == iota((NTM, EPAD), 0), 1.0, 0.0)
    before = jnp.where(iota((EPAD, EPAD), 0) < iota((EPAD, EPAD), 1), 1.0, 0.0).astype(BF16)
    ahead = jnp.dot(member.astype(BF16), before, preferred_element_type=F32)
    rank = jnp.sum(ahead * member, axis=0, keepdims=True).astype(jnp.int32)
    live = entry < jnp.minimum(live_ref[0, 0], ENT)
    place = jnp.where(live, target * CAP + rank, -1)

    taps[...] = jnp.zeros(taps.shape, F32)
    taps[0:1, 0:TAPS] = band_ref[...]
    line = jnp.broadcast_to(taps[0:1, :], (80, 128))
    parts = []
    for s in range(4):
        tap = iota((80, 128), 1) + 128 * s + DEC * iota((80, 128), 0) - (RECLEN - DEC)
        good = (tap >= 0) & (tap < TAPS) & (iota((80, 128), 0) < 72)
        parts.append(jnp.where(good, lane_take(line, jnp.clip(tap, 0, 127)), 0.0))
    band = jnp.concatenate(parts, axis=1)
    band_hi = band.astype(BF16)
    band_lo = (band - band_hi.astype(F32)).astype(BF16)

    rec_copy.wait()
    data = rec[...]
    data_hi = data.astype(BF16)
    data_lo = (data - data_hi.astype(F32)).astype(BF16)
    parts = lax.dot_general(band_hi, data_hi, NT, preferred_element_type=F32)
    parts += lax.dot_general(band_hi, data_lo, NT, preferred_element_type=F32)
    parts += lax.dot_general(band_lo, data_hi, NT, preferred_element_type=F32)
    row = iota((80, EPAD), 0)
    parts = jnp.where(row == 72, jnp.broadcast_to(chan.astype(F32), (80, EPAD)), parts)
    parts = jnp.where(row == 73, jnp.broadcast_to(slot.astype(F32), (80, EPAD)), parts)
    parts = jnp.concatenate([parts, jnp.zeros((48, EPAD), F32)], axis=0).astype(BF16)

    ybuf[NTM * CAP :, :] = jnp.zeros((CAP, 128), F32)
    for q in range(4):
        pick = jnp.where(
            jnp.broadcast_to(place, (256, EPAD)) == iota((256, EPAD), 0) + 256 * q, 1.0, 0.0
        ).astype(BF16)
        ybuf[256 * q : 256 * q + 256, :] = lax.dot_general(
            pick, parts, NT, preferred_element_type=F32
        )
    lane = iota((256, 128), 1)
    for q in range(4):
        own = ybuf[256 * q : 256 * q + 256, :]
        after = ybuf[256 * q + CAP : 256 * q + 256 + CAP, :]
        both = jnp.where((lane >= 80) & (lane < 90), pltpu.roll(after, 16, 1), own)
        send[16 * q : 16 * q + 16] = both.astype(BF16).reshape(16, CAP, 128)

    pl.semaphore_wait(barrier, 66 + jnp.where(me > 0, 3, 0))

    def block_copy(to, frm):
        return pltpu.make_async_remote_copy(
            src_ref=send.at[to, pl.ds(0, WIRE)],
            dst_ref=arr.at[frm, pl.ds(0, WIRE)],
            send_sem=a_send,
            recv_sem=a_recv,
            device_id={"tm": to},
            device_id_type=MESH,
        )

    x, z, core = me // 16, (me // 2) % 8, me % 2
    for dx, dz, dc in FAR_FIRST:
        to = ((x + dx) % 4) * 16 + ((z + dz) % 8) * 2 + (core + dc) % 2
        block_copy(to, me).start()
    arr[me] = send[me]

    def order_templates(b, _):
        tmpl_copy(b).wait()
        part = pl.ds(pl.multiple_of(b * 16, 16), 16)
        total = jnp.zeros((16, 16, 128), F32)
        for g in range(9):
            x = tmpl[part, 16 * g : 16 * g + 16, :]
            wts[16 * g : 16 * g + 16, part, :] = jnp.transpose(x, (1, 0, 2))
            wide = x.astype(F32)
            total = total + wide * wide
        tsq[part, :] = jnp.sum(total, axis=1)
        return 0

    lax.fori_loop(0, 16, order_templates, 0)
    mean = jnp.sum(tsq[...], axis=1, keepdims=True) * (1.0 / (CH * TLEN))
    by_tmpl[...] = jnp.broadcast_to(
        1.0 / (CH * TLEN * jnp.sqrt(mean + EPSILON)), (KEPT, 128)
    )

    def all_blocks():
        return pltpu.make_async_remote_copy(
            src_ref=send.at[pl.ds(0, NTM - 1), pl.ds(0, WIRE)],
            dst_ref=arr.at[pl.ds(0, NTM - 1), pl.ds(0, WIRE)],
            send_sem=a_send,
            recv_sem=a_recv,
            device_id={"tm": me},
            device_id_type=MESH,
        )

    all_blocks().wait_recv()

    came = arr[...].reshape(NTM * CAP, 128)
    sel_row = iota((8, 128), 0)
    sel_lane = iota((8, 128), 1)
    selector = (
        ((sel_row == 0) & (sel_lane == 72))
        | ((sel_row == 1) & (sel_lane == 73))
        | ((sel_row == 2) & (sel_lane == 88))
        | ((sel_row == 3) & (sel_lane == 89))
    )
    names = lax.dot_general(
        jnp.where(selector, 1.0, 0.0).astype(BF16), came, NT, preferred_element_type=F32
    ).astype(jnp.int32)
    spot = names[0:1, :] + 48 * (15 - names[1:2, :])
    spot_next = jnp.where(names[3:4, :] == 0, names[2:3, :], -1)
    lane = iota((48, 128), 1)
    pick = jnp.where(
        jnp.broadcast_to(spot_next, (48, 1024)) == iota((48, 1024), 0), 1.0, 0.0
    ).astype(BF16)
    carry = pltpu.roll(jnp.dot(pick, came, preferred_element_type=F32), 48, 1)
    for b in range(8):
        pick = jnp.where(
            jnp.broadcast_to(spot, (96, 1024)) == iota((96, 1024), 0) + 96 * b, 1.0, 0.0
        ).astype(BF16)
        got = jnp.dot(pick, came, preferred_element_type=F32)
        odd = pltpu.roll(got[48:96], 64, 1)
        block = (
            jnp.where(lane < 72, got[0:48], 0.0)
            + jnp.where(lane >= 64, odd, 0.0)
            + jnp.where(lane < 8, carry, 0.0)
        )
        carry = odd
        gall[my, :, :, 128 * (b + 1) : 128 * (b + 2)] = block.astype(BF16).reshape(UNITS, 16, 128)

    @pl.when(me == NTM - 1)
    def _():
        gall[:, :, :, 0:128] = jnp.zeros((NY, UNITS, 16, 128), BF16)

    def halo_copy(quarter, to_tm, to_y, k=0):
        return pltpu.make_async_remote_copy(
            src_ref=gall.at[quarter, :, :, pl.ds(WIN, 128)],
            dst_ref=gall.at[quarter, :, :, pl.ds(0, 128)],
            send_sem=b_send.at[4 + k],
            recv_sem=halo_recv.at[quarter],
            device_id={"tm": to_tm, "tmpl": to_y},
            device_id_type=MESH,
        )

    def main_copy(quarter, to_y, k=0):
        return pltpu.make_async_remote_copy(
            src_ref=gall.at[quarter, :, :, pl.ds(128, WIN)],
            dst_ref=gall.at[quarter, :, :, pl.ds(128, WIN)],
            send_sem=b_send.at[k],
            recv_sem=main_recv.at[quarter],
            device_id={"tmpl": to_y},
            device_id_type=MESH,
        )

    @pl.when(me > 0)
    def _():
        for i in (0, 1, 3, 2):
            halo_copy(my, me - 1, lax.rem(my + i, NY), i).start()

    for i in (1, 3, 2):
        main_copy(my, lax.rem(my + i, NY), i).start()

    def quarter_of(n):
        step = n // UNITS
        return lax.rem(my + lax.bitwise_xor(step, lax.shift_right_logical(step, 1)), NY)

    def arrive(n, mine):
        quarter = quarter_of(n)
        if not mine:
            main_copy(quarter, my).wait_recv()

        @pl.when(me < NTM - 1)
        def _():
            halo_copy(quarter, me, my).wait_recv()

    hl = iota((16, 128), 1)
    hr = iota((16, 128), 0)

    def build(n, side):
        wide = gall[quarter_of(n), lax.rem(n, UNITS)].astype(F32)
        g32[side] = wide
        pw[...] += wide * wide
        for i in range(UCH):
            line = [
                jnp.broadcast_to(g32[side, i : i + 1, 128 * b : 128 * b + 128], (16, 128))
                for b in range(9)
            ]
            for s in range(8):
                from_next = hl >= hr + 16 * s
                turned = [pltpu.roll(x, 16 * s, 1, stride=1, stride_axis=0) for x in line]
                for b in range(8):
                    at = i * 128 + 16 * s
                    hank[side, at : at + 16, 128 * b : 128 * b + 128] = jnp.where(
                        from_next, turned[b + 1], turned[b]
                    ).astype(BF16)

    def correlate(n, side):
        c0 = quarter_of(n) * (CH // NY) + lax.rem(n, UNITS) * UCH
        left = jnp.concatenate([wts[c0 + i] for i in range(UCH)], axis=1)
        acc[...] += jnp.dot(left, hank[side], preferred_element_type=F32)

    acc[...] = jnp.zeros(acc.shape, F32)
    pw[...] = jnp.zeros(pw.shape, F32)
    arrive(0, True)
    build(0, 0)
    total_units = NY * UNITS

    def step(it, _):
        n = 2 * it

        @pl.when((it == 1) | (it == 4))
        def _():
            arrive(n + 1, False)

        build(n + 1, 1)
        correlate(n, 0)

        @pl.when(it == 2)
        def _():
            arrive(n + 2, False)

        build(n + 2, 0)
        correlate(n + 1, 1)
        return 0

    lax.fori_loop(0, total_units // 2 - 1, step, 0)
    build(total_units - 1, 1)
    energy = jnp.broadcast_to(jnp.sum(pw[...], axis=0, keepdims=True), (8, WIN + 128))
    for k in (1, 2, 4, 8, 16, 32, 64):
        energy = energy + pltpu.roll(energy, k, 1)
    by_time[...] = 1.0 / jnp.sqrt(energy[:, 128:] * (1.0 / (CH * TLEN)) + EPSILON)
    correlate(total_units - 2, 0)
    correlate(total_units - 1, 1)

    all_blocks().wait_send()
    for i in range(1, NY):
        main_copy(my, lax.rem(my + i, NY), i).wait_send()

    @pl.when(me > 0)
    def _():
        for i in range(NY):
            halo_copy(my, me - 1, lax.rem(my + i, NY), i).wait_send()


def finish(acc, by_tmpl, by_time, out_hbm, stage, sem):
    back = 127 - iota((KEPT, 128), 1)
    copies = []
    for b in range(8):
        at = pl.ds(128 * (7 - b), 128)
        part = acc[:, 128 * b : 128 * b + 128] * by_tmpl[...]
        part = part * by_time[0:1, 128 * b : 128 * b + 128]
        stage[b] = lane_take(part, back)
        copies.append(pltpu.make_async_copy(stage.at[b], out_hbm.at[:, at], sem.at[b]))
        copies[-1].start()
    for copy in copies:
        copy.wait()


def in_hbm(x):
    return pltpu.with_memory_space_constraint(x, pltpu.HBM)


def shards(records, band_filter, templates, destinations, offsets, live_counts):
    vmem = pl.BlockSpec(memory_space=pltpu.VMEM)
    hbm = pl.BlockSpec(memory_space=pltpu.HBM)
    acc, by_tmpl, by_time = pl.pallas_call(
        kernel,
        out_shape=[
            jax.ShapeDtypeStruct((KEPT, WIN), F32),
            jax.ShapeDtypeStruct((KEPT, 128), F32),
            jax.ShapeDtypeStruct((8, WIN), F32),
        ],
        in_specs=[hbm, hbm, pl.BlockSpec(memory_space=pltpu.SMEM), hbm, hbm, hbm],
        out_specs=[vmem] * 3,
        scratch_shapes=[
            pltpu.VMEM((EPAD, RECLEN), F32),
            pltpu.VMEM((KEPT, CH, TLEN), BF16),
            pltpu.VMEM((8, 128), F32),
            pltpu.VMEM((8, EPAD), jnp.int32),
            pltpu.VMEM((NTM * CAP + CAP, 128), F32),
            pltpu.VMEM((NTM, CAP, 128), BF16),
            pltpu.VMEM((NTM, CAP, 128), BF16),
            pltpu.VMEM((CH, KEPT, TLEN), BF16),
            pltpu.VMEM((KEPT, 128), F32),
            pltpu.VMEM((NY, UNITS, 16, WIN + 128), BF16),
            pltpu.VMEM((2, 16, WIN + 128), F32),
            pltpu.VMEM((16, WIN + 128), F32),
            pltpu.VMEM((2, UCH * TLEN, WIN), BF16),
            pltpu.VMEM((1, ENT), jnp.int32),
            pltpu.VMEM((1, ENT), jnp.int32),
            pltpu.VMEM((1, TAPS), F32),
            pltpu.SemaphoreType.DMA((4,)),
            pltpu.SemaphoreType.DMA((16,)),
            pltpu.SemaphoreType.DMA,
            pltpu.SemaphoreType.DMA,
            pltpu.SemaphoreType.DMA((2 * NY,)),
            pltpu.SemaphoreType.DMA((NY,)),
            pltpu.SemaphoreType.DMA((NY,)),
        ],
        compiler_params=pltpu.CompilerParams(
            collective_id=0, has_side_effects=True, vmem_limit_bytes=52 * 1024 * 1024
        ),
    )(
        in_hbm(destinations),
        in_hbm(offsets),
        live_counts,
        in_hbm(band_filter.reshape(1, TAPS)),
        in_hbm(records),
        in_hbm(templates),
    )
    return pl.pallas_call(
        finish,
        out_shape=jax.ShapeDtypeStruct((KEPT, WIN), F32),
        in_specs=[vmem] * 3,
        out_specs=hbm,
        scratch_shapes=[pltpu.VMEM((8, KEPT, 128), F32), pltpu.SemaphoreType.DMA((8,))],
        compiler_params=pltpu.CompilerParams(vmem_limit_bytes=8 * 1024 * 1024),
    )(acc, by_tmpl, by_time)


def solution(mesh):
    in_specs = (
        P("tmpl", "tm", None),
        P(),
        P("tmpl", None, None),
        P("tmpl", "tm"),
        P("tmpl", "tm"),
        P("tmpl", "tm"),
    )
    return jax.shard_map(
        shards, mesh=mesh, in_specs=in_specs, out_specs=P("tmpl", "tm"), check_vma=False
    )
```

```python
import jax
import jax.numpy as jnp
from jax import lax
from jax.experimental import pallas as pl
from jax.experimental.pallas import tpu as pltpu
from jax.sharding import PartitionSpec as P

CH = 144
TAPS = 65
DEC = 8
RECLEN = 512
TLEN = 128
EPSILON = 1e-06

NTM = 64
NY = 4
ENT = 576
EPAD = 640
CAP = 16
WIRE = 10
UNITS = 3
UCH = 12
KEPT = 256
WIN = 1024
F32 = jnp.float32
BF16 = jnp.bfloat16
MESH = pl.DeviceIdType.MESH
FAR_FIRST = sorted(
    [(dx, dz, dc) for dx in range(4) for dz in range(8) for dc in range(2)][1:],
    key=lambda d: -(min(d[0], 4 - d[0]) + min(d[1], 8 - d[1])),
)
NT = (((1,), (1,)), ((), ()))


def iota(shape, dim):
    return lax.broadcasted_iota(jnp.int32, shape, dim)


def lane_take(x, index):
    return jnp.take_along_axis(x, index, axis=1)


def kernel(
    dest_hbm,
    offs_hbm,
    live_ref,
    band_hbm,
    rec_hbm,
    tmpl_hbm,
    acc,
    by_tmpl,
    by_time,
    rec,
    tmpl,
    taps,
    rows,
    ybuf,
    send,
    arr,
    wts,
    tsq,
    gall,
    g32,
    pw,
    hank,
    dest_ref,
    offs_ref,
    band_ref,
    rec_sem,
    tmpl_sem,
    a_send,
    a_recv,
    b_send,
    main_recv,
    halo_recv,
):
    me = lax.axis_index("tm")
    my = lax.axis_index("tmpl")

    rec_copy = pltpu.make_async_copy(rec_hbm.at[0], rec.at[pl.ds(0, ENT)], rec_sem.at[0])
    small = [
        pltpu.make_async_copy(dest_hbm, dest_ref, rec_sem.at[1]),
        pltpu.make_async_copy(offs_hbm, offs_ref, rec_sem.at[2]),
        pltpu.make_async_copy(band_hbm, band_ref, rec_sem.at[3]),
    ]
    for copy in small:
        copy.start()
    rec_copy.start()
    arr[...] = jnp.zeros(arr.shape, BF16)
    barrier = pltpu.get_barrier_semaphore()

    def greet(i, _):
        pl.semaphore_signal(
            barrier, inc=1, device_id={"tm": lax.rem(me + i, NTM)}, device_id_type=MESH
        )
        return 0

    lax.fori_loop(1, NTM, greet, 0)
    for i in range(1, NY):
        other = lax.rem(my + i, NY)
        pl.semaphore_signal(barrier, inc=1, device_id={"tmpl": other}, device_id_type=MESH)

        @pl.when(me < NTM - 1)
        def _():
            pl.semaphore_signal(
                barrier, inc=1, device_id={"tm": me + 1, "tmpl": other}, device_id_type=MESH
            )

    def tmpl_copy(b):
        part = pl.ds(pl.multiple_of(b * 16, 16), 16)
        return pltpu.make_async_copy(tmpl_hbm.at[part], tmpl.at[part], tmpl_sem.at[b])

    for b in range(16):
        tmpl_copy(b).start()

    rec[ENT:EPAD, :] = jnp.zeros((EPAD - ENT, RECLEN), F32)
    rows[...] = jnp.full(rows.shape, -1, jnp.int32)
    for copy in small:
        copy.wait()
    rows[0:1, 0:ENT] = dest_ref[...]
    rows[1:2, 0:ENT] = offs_ref[...]
    entry = iota((1, EPAD), 1)
    target = rows[0:1, :]
    label = jnp.maximum(rows[1:2, :], 0) // RECLEN
    chan = label // 16
    slot = label - chan * 16
    chan = chan + 4 * (chan // UCH)
    member = jnp.where(jnp.broadcast_to(target, (NTM, EPAD)) == iota((NTM, EPAD), 0), 1.0, 0.0)
    before = jnp.where(iota((EPAD, EPAD), 0) < iota((EPAD, EPAD), 1), 1.0, 0.0).astype(BF16)
    ahead = jnp.dot(member.astype(BF16), before, preferred_element_type=F32)
    rank = jnp.sum(ahead * member, axis=0, keepdims=True).astype(jnp.int32)
    live = entry < jnp.minimum(live_ref[0, 0], ENT)
    place = jnp.where(live, target * CAP + rank, -1)

    taps[...] = jnp.zeros(taps.shape, F32)
    taps[0:1, 0:TAPS] = band_ref[...]
    line = jnp.broadcast_to(taps[0:1, :], (80, 128))
    parts = []
    for s in range(4):
        tap = iota((80, 128), 1) + 128 * s + DEC * iota((80, 128), 0) - (RECLEN - DEC)
        good = (tap >= 0) & (tap < TAPS) & (iota((80, 128), 0) < 72)
        parts.append(jnp.where(good, lane_take(line, jnp.clip(tap, 0, 127)), 0.0))
    band = jnp.concatenate(parts, axis=1)
    band_hi = band.astype(BF16)
    band_lo = (band - band_hi.astype(F32)).astype(BF16)

    rec_copy.wait()
    data = rec[...]
    data_hi = data.astype(BF16)
    data_lo = (data - data_hi.astype(F32)).astype(BF16)
    parts = lax.dot_general(band_hi, data_hi, NT, preferred_element_type=F32)
    parts += lax.dot_general(band_hi, data_lo, NT, preferred_element_type=F32)
    parts += lax.dot_general(band_lo, data_hi, NT, preferred_element_type=F32)
    row = iota((80, EPAD), 0)
    parts = jnp.where(row == 72, jnp.broadcast_to(chan.astype(F32), (80, EPAD)), parts)
    parts = jnp.where(row == 73, jnp.broadcast_to(slot.astype(F32), (80, EPAD)), parts)
    parts = jnp.concatenate([parts, jnp.zeros((48, EPAD), F32)], axis=0).astype(BF16)

    ybuf[NTM * CAP :, :] = jnp.zeros((CAP, 128), F32)
    for q in range(4):
        pick = jnp.where(
            jnp.broadcast_to(place, (256, EPAD)) == iota((256, EPAD), 0) + 256 * q, 1.0, 0.0
        ).astype(BF16)
        ybuf[256 * q : 256 * q + 256, :] = lax.dot_general(
            pick, parts, NT, preferred_element_type=F32
        )
    lane = iota((256, 128), 1)
    for q in range(4):
        own = ybuf[256 * q : 256 * q + 256, :]
        after = ybuf[256 * q + CAP : 256 * q + 256 + CAP, :]
        both = jnp.where((lane >= 80) & (lane < 90), pltpu.roll(after, 16, 1), own)
        send[16 * q : 16 * q + 16] = both.astype(BF16).reshape(16, CAP, 128)

    pl.semaphore_wait(barrier, 66 + jnp.where(me > 0, 3, 0))

    def block_copy(to, frm):
        return pltpu.make_async_remote_copy(
            src_ref=send.at[to, pl.ds(0, WIRE)],
            dst_ref=arr.at[frm, pl.ds(0, WIRE)],
            send_sem=a_send,
            recv_sem=a_recv,
            device_id={"tm": to},
            device_id_type=MESH,
        )

    x, z, core = me // 16, (me // 2) % 8, me % 2
    for dx, dz, dc in FAR_FIRST:
        to = ((x + dx) % 4) * 16 + ((z + dz) % 8) * 2 + (core + dc) % 2
        block_copy(to, me).start()
    arr[me] = send[me]

    def order_templates(b, _):
        tmpl_copy(b).wait()
        part = pl.ds(pl.multiple_of(b * 16, 16), 16)
        total = jnp.zeros((16, 16, 128), F32)
        for g in range(9):
            x = tmpl[part, 16 * g : 16 * g + 16, :]
            wts[16 * g : 16 * g + 16, part, :] = jnp.transpose(x, (1, 0, 2))
            wide = x.astype(F32)
            total = total + wide * wide
        tsq[part, :] = jnp.sum(total, axis=1)
        return 0

    lax.fori_loop(0, 16, order_templates, 0)
    mean = jnp.sum(tsq[...], axis=1, keepdims=True) * (1.0 / (CH * TLEN))
    by_tmpl[...] = jnp.broadcast_to(
        1.0 / (CH * TLEN * jnp.sqrt(mean + EPSILON)), (KEPT, 128)
    )

    def all_blocks():
        return pltpu.make_async_remote_copy(
            src_ref=send.at[pl.ds(0, NTM - 1), pl.ds(0, WIRE)],
            dst_ref=arr.at[pl.ds(0, NTM - 1), pl.ds(0, WIRE)],
            send_sem=a_send,
            recv_sem=a_recv,
            device_id={"tm": me},
            device_id_type=MESH,
        )

    all_blocks().wait_recv()

    came = arr[...].reshape(NTM * CAP, 128)
    sel_row = iota((8, 128), 0)
    sel_lane = iota((8, 128), 1)
    selector = (
        ((sel_row == 0) & (sel_lane == 72))
        | ((sel_row == 1) & (sel_lane == 73))
        | ((sel_row == 2) & (sel_lane == 88))
        | ((sel_row == 3) & (sel_lane == 89))
    )
    names = lax.dot_general(
        jnp.where(selector, 1.0, 0.0).astype(BF16), came, NT, preferred_element_type=F32
    ).astype(jnp.int32)
    spot = names[0:1, :] + 48 * (15 - names[1:2, :])
    spot_next = jnp.where(names[3:4, :] == 0, names[2:3, :], -1)
    lane = iota((48, 128), 1)
    pick = jnp.where(
        jnp.broadcast_to(spot_next, (48, 1024)) == iota((48, 1024), 0), 1.0, 0.0
    ).astype(BF16)
    carry = pltpu.roll(jnp.dot(pick, came, preferred_element_type=F32), 48, 1)
    for b in range(8):
        pick = jnp.where(
            jnp.broadcast_to(spot, (96, 1024)) == iota((96, 1024), 0) + 96 * b, 1.0, 0.0
        ).astype(BF16)
        got = jnp.dot(pick, came, preferred_element_type=F32)
        odd = pltpu.roll(got[48:96], 64, 1)
        block = (
            jnp.where(lane < 72, got[0:48], 0.0)
            + jnp.where(lane >= 64, odd, 0.0)
            + jnp.where(lane < 8, carry, 0.0)
        )
        carry = odd
        gall[my, :, b + 1] = block.astype(BF16).reshape(UNITS, 16, 128)

    @pl.when(me == NTM - 1)
    def _():
        gall[:, :, 0] = jnp.zeros((NY, UNITS, 16, 128), BF16)

    def halo_copy(quarter, to_tm, to_y, k=0):
        return pltpu.make_async_remote_copy(
            src_ref=gall.at[quarter, :, 8, pl.ds(0, UCH)],
            dst_ref=gall.at[quarter, :, 0, pl.ds(0, UCH)],
            send_sem=b_send.at[4 + k],
            recv_sem=halo_recv.at[quarter],
            device_id={"tm": to_tm, "tmpl": to_y},
            device_id_type=MESH,
        )

    def main_copy(quarter, to_y, k=0):
        return pltpu.make_async_remote_copy(
            src_ref=gall.at[quarter, :, pl.ds(1, 8), pl.ds(0, UCH)],
            dst_ref=gall.at[quarter, :, pl.ds(1, 8), pl.ds(0, UCH)],
            send_sem=b_send.at[k],
            recv_sem=main_recv.at[quarter],
            device_id={"tmpl": to_y},
            device_id_type=MESH,
        )

    @pl.when(me > 0)
    def _():
        for i in (0, 1, 3, 2):
            halo_copy(my, me - 1, lax.rem(my + i, NY), i).start()

    for i in (1, 3):
        main_copy(my, lax.rem(my + i, NY), i).start()

    def quarter_of(n):
        step = n // UNITS
        return lax.rem(my + lax.bitwise_xor(step, lax.shift_right_logical(step, 1)), NY)

    def arrive(n, mine):
        quarter = quarter_of(n)
        if not mine:
            main_copy(quarter, my).wait_recv()

        @pl.when(me < NTM - 1)
        def _():
            halo_copy(quarter, me, my).wait_recv()

    hl = iota((16, 128), 1)
    hr = iota((16, 128), 0)

    def widen(n, side, first, last):
        for b in range(first, last):
            at = slice(128 * b, 128 * b + 128)
            wide = gall[quarter_of(n), lax.rem(n, UNITS), b].astype(F32)
            wide = jnp.where(hr < UCH, wide, 0.0)
            g32[side, :, at] = wide
            pw[:, at] += wide * wide

    def expand(side, channels, first, last):
        for i in channels:
            line = [
                jnp.broadcast_to(g32[side, i : i + 1, 128 * b : 128 * b + 128], (16, 128))
                for b in range(first, last + 1)
            ]
            for s in range(8):
                from_next = hl >= hr + 16 * s
                turned = [pltpu.roll(x, 16 * s, 1, stride=1, stride_axis=0) for x in line]
                for b in range(first, last):
                    at = i * 128 + 16 * s
                    hank[side, at : at + 16, 128 * b : 128 * b + 128] = jnp.where(
                        from_next, turned[b - first + 1], turned[b - first]
                    ).astype(BF16)

    def build(n, side):
        widen(n, side, 0, 9)
        expand(side, range(UCH), 0, 8)

    def correlate(n, side, lo=0, hi=WIN, channels=range(UCH)):
        c0 = quarter_of(n) * (CH // NY) + lax.rem(n, UNITS) * UCH
        left = jnp.concatenate([wts[c0 + i] for i in channels], axis=1)
        deep = slice(channels[0] * TLEN, (channels[-1] + 1) * TLEN)
        acc[:, lo:hi] += jnp.dot(left, hank[side, deep, lo:hi], preferred_element_type=F32)

    acc[...] = jnp.zeros(acc.shape, F32)
    pw[...] = jnp.zeros(pw.shape, F32)
    widen(0, 0, 1, 9)
    thirds = [range(4 * i, 4 * i + 4) for i in range(3)]
    expand(0, thirds[0], 1, 8)
    for i in range(3):
        if i < 2:
            expand(0, thirds[i + 1], 1, 8)
        correlate(0, 0, 256, WIN, thirds[i])
    arrive(0, True)
    widen(0, 0, 0, 1)
    expand(0, range(UCH), 0, 1)
    build(1, 1)
    correlate(0, 0, 0, 256)
    main_copy(my, lax.rem(my + 2, NY), 2).start()
    build(2, 0)
    correlate(1, 1)
    total_units = NY * UNITS

    def step(it, _):
        n = 2 * it

        @pl.when((it == 1) | (it == 4))
        def _():
            arrive(n + 1, False)

        build(n + 1, 1)
        correlate(n, 0)

        @pl.when(it == 2)
        def _():
            arrive(n + 2, False)

        build(n + 2, 0)
        correlate(n + 1, 1)
        return 0

    lax.fori_loop(1, total_units // 2 - 1, step, 0)
    build(total_units - 1, 1)
    energy = jnp.broadcast_to(jnp.sum(pw[...], axis=0, keepdims=True), (8, WIN + 128))
    for k in (1, 2, 4, 8, 16, 32, 64):
        energy = energy + pltpu.roll(energy, k, 1)
    by_time[...] = 1.0 / jnp.sqrt(energy[:, 128:] * (1.0 / (CH * TLEN)) + EPSILON)
    correlate(total_units - 2, 0)
    correlate(total_units - 1, 1)

    all_blocks().wait_send()
    for i in range(1, NY):
        main_copy(my, lax.rem(my + i, NY), i).wait_send()

    @pl.when(me > 0)
    def _():
        for i in range(NY):
            halo_copy(my, me - 1, lax.rem(my + i, NY), i).wait_send()


def finish(acc, by_tmpl, by_time, out_hbm, stage, sem):
    back = 127 - iota((KEPT, 128), 1)
    copies = []
    for b in range(8):
        at = pl.ds(128 * (7 - b), 128)
        part = acc[:, 128 * b : 128 * b + 128] * by_tmpl[...]
        part = part * by_time[0:1, 128 * b : 128 * b + 128]
        stage[b] = lane_take(part, back)
        copies.append(pltpu.make_async_copy(stage.at[b], out_hbm.at[:, at], sem.at[b]))
        copies[-1].start()
    for copy in copies:
        copy.wait()


def in_hbm(x):
    return pltpu.with_memory_space_constraint(x, pltpu.HBM)


def shards(records, band_filter, templates, destinations, offsets, live_counts):
    vmem = pl.BlockSpec(memory_space=pltpu.VMEM)
    hbm = pl.BlockSpec(memory_space=pltpu.HBM)
    acc, by_tmpl, by_time = pl.pallas_call(
        kernel,
        out_shape=[
            jax.ShapeDtypeStruct((KEPT, WIN), F32),
            jax.ShapeDtypeStruct((KEPT, 128), F32),
            jax.ShapeDtypeStruct((8, WIN), F32),
        ],
        in_specs=[hbm, hbm, pl.BlockSpec(memory_space=pltpu.SMEM), hbm, hbm, hbm],
        out_specs=[vmem] * 3,
        scratch_shapes=[
            pltpu.VMEM((EPAD, RECLEN), F32),
            pltpu.VMEM((KEPT, CH, TLEN), BF16),
            pltpu.VMEM((8, 128), F32),
            pltpu.VMEM((8, EPAD), jnp.int32),
            pltpu.VMEM((NTM * CAP + CAP, 128), F32),
            pltpu.VMEM((NTM, CAP, 128), BF16),
            pltpu.VMEM((NTM, CAP, 128), BF16),
            pltpu.VMEM((CH, KEPT, TLEN), BF16),
            pltpu.VMEM((KEPT, 128), F32),
            pltpu.VMEM((NY, UNITS, 9, 16, 128), BF16),
            pltpu.VMEM((2, 16, WIN + 128), F32),
            pltpu.VMEM((16, WIN + 128), F32),
            pltpu.VMEM((2, UCH * TLEN, WIN), BF16),
            pltpu.VMEM((1, ENT), jnp.int32),
            pltpu.VMEM((1, ENT), jnp.int32),
            pltpu.VMEM((1, TAPS), F32),
            pltpu.SemaphoreType.DMA((4,)),
            pltpu.SemaphoreType.DMA((16,)),
            pltpu.SemaphoreType.DMA,
            pltpu.SemaphoreType.DMA,
            pltpu.SemaphoreType.DMA((2 * NY,)),
            pltpu.SemaphoreType.DMA((NY,)),
            pltpu.SemaphoreType.DMA((NY,)),
        ],
        compiler_params=pltpu.CompilerParams(
            collective_id=0, has_side_effects=True, vmem_limit_bytes=52 * 1024 * 1024
        ),
    )(
        in_hbm(destinations),
        in_hbm(offsets),
        live_counts,
        in_hbm(band_filter.reshape(1, TAPS)),
        in_hbm(records),
        in_hbm(templates),
    )
    return pl.pallas_call(
        finish,
        out_shape=jax.ShapeDtypeStruct((KEPT, WIN), F32),
        in_specs=[vmem] * 3,
        out_specs=hbm,
        scratch_shapes=[pltpu.VMEM((8, KEPT, 128), F32), pltpu.SemaphoreType.DMA((8,))],
        compiler_params=pltpu.CompilerParams(vmem_limit_bytes=8 * 1024 * 1024),
    )(acc, by_tmpl, by_time)


def solution(mesh):
    in_specs = (
        P("tmpl", "tm", None),
        P(),
        P("tmpl", None, None),
        P("tmpl", "tm"),
        P("tmpl", "tm"),
        P("tmpl", "tm"),
    )
    return jax.shard_map(
        shards, mesh=mesh, in_specs=in_specs, out_specs=P("tmpl", "tm"), check_vma=False
    )
```

```python
import jax
import jax.numpy as jnp
from jax import lax
from jax.experimental import pallas as pl
from jax.experimental.pallas import tpu as pltpu
from jax.sharding import PartitionSpec as P

CH = 144
TAPS = 65
DEC = 8
RECLEN = 512
TLEN = 128
EPSILON = 1e-06

NTM = 64
NY = 4
ENT = 576
EPAD = 640
CAP = 16
WIRE = 10
UNITS = 3
UCH = 12
KEPT = 256
WIN = 1024
F32 = jnp.float32
BF16 = jnp.bfloat16
MESH = pl.DeviceIdType.MESH
FAR_FIRST = sorted(
    [(dx, dz, dc) for dx in range(4) for dz in range(8) for dc in range(2)][1:],
    key=lambda d: -(min(d[0], 4 - d[0]) + min(d[1], 8 - d[1])),
)
NT = (((1,), (1,)), ((), ()))


def iota(shape, dim):
    return lax.broadcasted_iota(jnp.int32, shape, dim)


def lane_take(x, index):
    return jnp.take_along_axis(x, index, axis=1)


def kernel(
    dest_hbm,
    offs_hbm,
    live_ref,
    band_hbm,
    rec_hbm,
    tmpl_hbm,
    acc,
    by_tmpl,
    by_time,
    hank1,
    last_wts,
    rec,
    tmpl,
    taps,
    rows,
    ybuf,
    send,
    arr,
    wts,
    tsq,
    gall,
    g32,
    pw,
    hank0,
    dest_ref,
    offs_ref,
    band_ref,
    rec_sem,
    tmpl_sem,
    a_send,
    a_recv,
    b_send,
    main_recv,
    halo_recv,
):
    me = lax.axis_index("tm")
    my = lax.axis_index("tmpl")

    rec_copy = pltpu.make_async_copy(rec_hbm.at[0], rec.at[pl.ds(0, ENT)], rec_sem.at[0])
    small = [
        pltpu.make_async_copy(dest_hbm, dest_ref, rec_sem.at[1]),
        pltpu.make_async_copy(offs_hbm, offs_ref, rec_sem.at[2]),
        pltpu.make_async_copy(band_hbm, band_ref, rec_sem.at[3]),
    ]
    for copy in small:
        copy.start()
    rec_copy.start()
    arr[...] = jnp.zeros(arr.shape, BF16)
    barrier = pltpu.get_barrier_semaphore()

    x, z, core = me // 16, (me // 2) % 8, me % 2
    partners = [
        ((x + dx) % 4) * 16 + ((z + dz) % 8) * 2 + (core + dc) % 2 for dx, dz, dc in FAR_FIRST
    ]
    for to in partners:
        pl.semaphore_signal(barrier, inc=1, device_id={"tm": to}, device_id_type=MESH)
    for i in range(1, NY):
        other = lax.rem(my + i, NY)
        pl.semaphore_signal(barrier, inc=1, device_id={"tmpl": other}, device_id_type=MESH)

        @pl.when(me < NTM - 1)
        def _():
            pl.semaphore_signal(
                barrier, inc=1, device_id={"tm": me + 1, "tmpl": other}, device_id_type=MESH
            )

    def tmpl_copy(b):
        part = pl.ds(pl.multiple_of(b * 16, 16), 16)
        return pltpu.make_async_copy(tmpl_hbm.at[part], tmpl.at[part], tmpl_sem.at[b])

    for b in range(16):
        tmpl_copy(b).start()

    rec[ENT:EPAD, :] = jnp.zeros((EPAD - ENT, RECLEN), F32)
    rows[...] = jnp.full(rows.shape, -1, jnp.int32)
    for copy in small:
        copy.wait()
    rows[0:1, 0:ENT] = dest_ref[...]
    rows[1:2, 0:ENT] = offs_ref[...]
    entry = iota((1, EPAD), 1)
    target = rows[0:1, :]
    label = jnp.maximum(rows[1:2, :], 0) // RECLEN
    chan = label // 16
    slot = label - chan * 16
    chan = chan + 4 * (chan // UCH)
    member = jnp.where(jnp.broadcast_to(target, (NTM, EPAD)) == iota((NTM, EPAD), 0), 1.0, 0.0)
    before = jnp.where(iota((EPAD, EPAD), 0) < iota((EPAD, EPAD), 1), 1.0, 0.0).astype(BF16)
    ahead = jnp.dot(member.astype(BF16), before, preferred_element_type=F32)
    rank = jnp.sum(ahead * member, axis=0, keepdims=True).astype(jnp.int32)
    live = entry < jnp.minimum(live_ref[0, 0], ENT)
    place = jnp.where(live, target * CAP + rank, -1)

    taps[...] = jnp.zeros(taps.shape, F32)
    taps[0:1, 0:TAPS] = band_ref[...]
    line = jnp.broadcast_to(taps[0:1, :], (80, 128))
    parts = []
    for s in range(4):
        tap = iota((80, 128), 1) + 128 * s + DEC * iota((80, 128), 0) - (RECLEN - DEC)
        good = (tap >= 0) & (tap < TAPS) & (iota((80, 128), 0) < 72)
        parts.append(jnp.where(good, lane_take(line, jnp.clip(tap, 0, 127)), 0.0))
    band = jnp.concatenate(parts, axis=1)
    band_hi = band.astype(BF16)
    band_lo = (band - band_hi.astype(F32)).astype(BF16)

    rec_copy.wait()
    data = rec[...]
    data_hi = data.astype(BF16)
    data_lo = (data - data_hi.astype(F32)).astype(BF16)
    both = jnp.concatenate([band_hi, band_lo], axis=0)
    both = lax.dot_general(both, data_hi, NT, preferred_element_type=F32)
    parts = lax.dot_general(band_hi, data_lo, NT, preferred_element_type=F32)
    parts += both[0:80] + both[80:160]
    row = iota((80, EPAD), 0)
    parts = jnp.where(row == 72, jnp.broadcast_to(chan.astype(F32), (80, EPAD)), parts)
    parts = jnp.where(row == 73, jnp.broadcast_to(slot.astype(F32), (80, EPAD)), parts)
    parts = jnp.concatenate([parts, jnp.zeros((48, EPAD), F32)], axis=0).astype(BF16)

    ybuf[NTM * CAP :, :] = jnp.zeros((CAP, 128), F32)
    for q in range(4):
        pick = jnp.where(
            jnp.broadcast_to(place, (256, EPAD)) == iota((256, EPAD), 0) + 256 * q, 1.0, 0.0
        ).astype(BF16)
        ybuf[256 * q : 256 * q + 256, :] = lax.dot_general(
            pick, parts, NT, preferred_element_type=F32
        )
    lane = iota((256, 128), 1)
    for q in range(4):
        own = ybuf[256 * q : 256 * q + 256, :]
        after = ybuf[256 * q + CAP : 256 * q + 256 + CAP, :]
        both = jnp.where((lane >= 80) & (lane < 90), pltpu.roll(after, 16, 1), own)
        send[16 * q : 16 * q + 16] = both.astype(BF16).reshape(16, CAP, 128)

    pl.semaphore_wait(barrier, 66 + jnp.where(me > 0, 3, 0))

    def block_copy(to, frm):
        return pltpu.make_async_remote_copy(
            src_ref=send.at[to, pl.ds(0, WIRE)],
            dst_ref=arr.at[frm, pl.ds(0, WIRE)],
            send_sem=a_send,
            recv_sem=a_recv,
            device_id={"tm": to},
            device_id_type=MESH,
        )

    for to in partners:
        block_copy(to, me).start()
    arr[me] = send[me]

    def order_templates(b, _):
        tmpl_copy(b).wait()
        part = pl.ds(pl.multiple_of(b * 16, 16), 16)
        total = jnp.zeros((16, 16, 128), F32)
        for g in range(9):
            x = tmpl[part, 16 * g : 16 * g + 16, :]
            wts[16 * g : 16 * g + 16, part, :] = jnp.transpose(x, (1, 0, 2))
            wide = x.astype(F32)
            total = total + wide * wide
        tsq[part, :] = jnp.sum(total, axis=1)
        return 0

    lax.fori_loop(0, 16, order_templates, 0)
    mean = jnp.sum(tsq[...], axis=1, keepdims=True) * (1.0 / (CH * TLEN))
    by_tmpl[...] = jnp.broadcast_to(
        1.0 / (CH * TLEN * jnp.sqrt(mean + EPSILON)), (KEPT, 128)
    )

    def all_blocks():
        return pltpu.make_async_remote_copy(
            src_ref=send.at[pl.ds(0, NTM - 1), pl.ds(0, WIRE)],
            dst_ref=arr.at[pl.ds(0, NTM - 1), pl.ds(0, WIRE)],
            send_sem=a_send,
            recv_sem=a_recv,
            device_id={"tm": me},
            device_id_type=MESH,
        )

    all_blocks().wait_recv()

    came = arr[...].reshape(NTM * CAP, 128)
    sel_row = iota((8, 128), 0)
    sel_lane = iota((8, 128), 1)
    selector = (
        ((sel_row == 0) & (sel_lane == 72))
        | ((sel_row == 1) & (sel_lane == 73))
        | ((sel_row == 2) & (sel_lane == 88))
        | ((sel_row == 3) & (sel_lane == 89))
    )
    names = lax.dot_general(
        jnp.where(selector, 1.0, 0.0).astype(BF16), came, NT, preferred_element_type=F32
    ).astype(jnp.int32)
    spot = names[0:1, :] + 48 * (15 - names[1:2, :])
    spot_next = jnp.where(names[3:4, :] == 0, names[2:3, :], -1)
    lane = iota((48, 128), 1)
    pick = jnp.where(
        jnp.broadcast_to(spot_next, (48, 1024)) == iota((48, 1024), 0), 1.0, 0.0
    ).astype(BF16)
    carry = pltpu.roll(jnp.dot(pick, came, preferred_element_type=F32), 48, 1)
    for b in range(8):
        pick = jnp.where(
            jnp.broadcast_to(spot, (96, 1024)) == iota((96, 1024), 0) + 96 * b, 1.0, 0.0
        ).astype(BF16)
        got = jnp.dot(pick, came, preferred_element_type=F32)
        odd = pltpu.roll(got[48:96], 64, 1)
        block = (
            jnp.where(lane < 72, got[0:48], 0.0)
            + jnp.where(lane >= 64, odd, 0.0)
            + jnp.where(lane < 8, carry, 0.0)
        )
        carry = odd
        gall[my, :, b + 1] = block.astype(BF16).reshape(UNITS, 16, 128)

    @pl.when(me == NTM - 1)
    def _():
        gall[:, :, 0] = jnp.zeros((NY, UNITS, 16, 128), BF16)

    def halo_copy(quarter, to_tm, to_y, k=0):
        return pltpu.make_async_remote_copy(
            src_ref=gall.at[quarter, :, 8, pl.ds(0, UCH)],
            dst_ref=gall.at[quarter, :, 0, pl.ds(0, UCH)],
            send_sem=b_send.at[4 + k],
            recv_sem=halo_recv.at[quarter],
            device_id={"tm": to_tm, "tmpl": to_y},
            device_id_type=MESH,
        )

    def main_copy(quarter, to_y, k=0):
        return pltpu.make_async_remote_copy(
            src_ref=gall.at[quarter, :, pl.ds(1, 8), pl.ds(0, UCH)],
            dst_ref=gall.at[quarter, :, pl.ds(1, 8), pl.ds(0, UCH)],
            send_sem=b_send.at[k],
            recv_sem=main_recv.at[quarter],
            device_id={"tmpl": to_y},
            device_id_type=MESH,
        )

    @pl.when(me > 0)
    def _():
        for i in (0, 1, 3, 2):
            halo_copy(my, me - 1, lax.rem(my + i, NY), i).start()

    for i in (1, 3):
        main_copy(my, lax.rem(my + i, NY), i).start()

    def quarter_of(n):
        step = n // UNITS
        return lax.rem(my + lax.bitwise_xor(step, lax.shift_right_logical(step, 1)), NY)

    def arrive(n, mine):
        quarter = quarter_of(n)
        if not mine:
            main_copy(quarter, my).wait_recv()

        @pl.when(me < NTM - 1)
        def _():
            halo_copy(quarter, me, my).wait_recv()

    hank = (hank0, hank1)
    last = NY * UNITS - 1
    hl = iota((16, 128), 1)
    hr = iota((16, 128), 0)

    def widen(n, side, first, last):
        for b in range(first, last):
            at = slice(128 * b, 128 * b + 128)
            wide = gall[quarter_of(n), lax.rem(n, UNITS), b].astype(F32)
            wide = jnp.where(hr < UCH, wide, 0.0)
            g32[side, :, at] = wide
            pw[:, at] += wide * wide

    def expand(side, channels, first, last):
        for i in channels:
            line = [
                jnp.broadcast_to(g32[side, i : i + 1, 128 * b : 128 * b + 128], (16, 128))
                for b in range(first, last + 1)
            ]
            for s in range(8):
                from_next = hl >= hr + 16 * s
                turned = [pltpu.roll(x, 16 * s, 1, stride=1, stride_axis=0) for x in line]
                for b in range(first, last):
                    at = i * 128 + 16 * s
                    hank[side][at : at + 16, 128 * b : 128 * b + 128] = jnp.where(
                        from_next, turned[b - first + 1], turned[b - first]
                    ).astype(BF16)

    def build(n, side):
        widen(n, side, 0, 9)
        expand(side, range(UCH), 0, 8)

    def correlate(n, side, lo=0, hi=WIN, channels=range(UCH)):
        c0 = quarter_of(n) * (CH // NY) + lax.rem(n, UNITS) * UCH
        left = jnp.concatenate([wts[c0 + i] for i in channels], axis=1)
        if n is last:
            last_wts[...] = left
            return
        deep = slice(channels[0] * TLEN, (channels[-1] + 1) * TLEN)
        acc[:, lo:hi] += jnp.dot(
            left, hank[side][deep, lo:hi], preferred_element_type=F32
        )

    acc[...] = jnp.zeros(acc.shape, F32)
    pw[...] = jnp.zeros(pw.shape, F32)
    widen(0, 0, 1, 9)
    thirds = [range(4 * i, 4 * i + 4) for i in range(3)]
    expand(0, thirds[0], 1, 8)
    for i in range(3):
        if i < 2:
            expand(0, thirds[i + 1], 1, 8)
        correlate(0, 0, 256, WIN, thirds[i])
    arrive(0, True)
    widen(0, 0, 0, 1)
    expand(0, range(UCH), 0, 1)
    build(1, 1)
    correlate(0, 0, 0, 256)
    main_copy(my, lax.rem(my + 2, NY), 2).start()
    build(2, 0)
    correlate(1, 1)

    def step(it, _):
        n = 2 * it

        @pl.when((it == 1) | (it == 4))
        def _():
            arrive(n + 1, False)

        build(n + 1, 1)
        correlate(n, 0)

        @pl.when(it == 2)
        def _():
            arrive(n + 2, False)

        build(n + 2, 0)
        correlate(n + 1, 1)
        return 0

    lax.fori_loop(1, NY * UNITS // 2 - 1, step, 0)
    build(last, 1)
    energy = jnp.broadcast_to(jnp.sum(pw[...], axis=0, keepdims=True), (8, WIN + 128))
    for k in (1, 2, 4, 8, 16, 32, 64):
        energy = energy + pltpu.roll(energy, k, 1)
    by_time[...] = 1.0 / jnp.sqrt(energy[:, 128:] * (1.0 / (CH * TLEN)) + EPSILON)
    correlate(last - 1, 0)
    correlate(last, 1)

    all_blocks().wait_send()
    for i in range(1, NY):
        main_copy(my, lax.rem(my + i, NY), i).wait_send()

    @pl.when(me > 0)
    def _():
        for i in range(NY):
            halo_copy(my, me - 1, lax.rem(my + i, NY), i).wait_send()


def finish(acc, by_tmpl, by_time, hank, wts, out_hbm, stage, sem):
    back = 127 - iota((KEPT, 128), 1)
    copies = []
    for two in range(4):
        span = slice(256 * two, 256 * two + 256)
        corr = acc[:, span] + jnp.dot(wts[...], hank[:, span], preferred_element_type=F32)
        for half in range(2):
            b = 2 * two + half
            part = corr[:, 128 * half : 128 * half + 128] * by_tmpl[...]
            part = part * by_time[0:1, 128 * b : 128 * b + 128]
            stage[b] = lane_take(part, back)
            at = pl.ds(128 * (7 - b), 128)
            copies.append(pltpu.make_async_copy(stage.at[b], out_hbm.at[:, at], sem.at[b]))
            copies[-1].start()
    for copy in copies:
        copy.wait()


def in_hbm(x):
    return pltpu.with_memory_space_constraint(x, pltpu.HBM)


def shards(records, band_filter, templates, destinations, offsets, live_counts):
    vmem = pl.BlockSpec(memory_space=pltpu.VMEM)
    hbm = pl.BlockSpec(memory_space=pltpu.HBM)
    results = pl.pallas_call(
        kernel,
        out_shape=[
            jax.ShapeDtypeStruct((KEPT, WIN), F32),
            jax.ShapeDtypeStruct((KEPT, 128), F32),
            jax.ShapeDtypeStruct((8, WIN), F32),
            jax.ShapeDtypeStruct((UCH * TLEN, WIN), BF16),
            jax.ShapeDtypeStruct((KEPT, UCH * TLEN), BF16),
        ],
        in_specs=[hbm, hbm, pl.BlockSpec(memory_space=pltpu.SMEM), hbm, hbm, hbm],
        out_specs=[vmem] * 5,
        scratch_shapes=[
            pltpu.VMEM((EPAD, RECLEN), F32),
            pltpu.VMEM((KEPT, CH, TLEN), BF16),
            pltpu.VMEM((8, 128), F32),
            pltpu.VMEM((8, EPAD), jnp.int32),
            pltpu.VMEM((NTM * CAP + CAP, 128), F32),
            pltpu.VMEM((NTM, CAP, 128), BF16),
            pltpu.VMEM((NTM, CAP, 128), BF16),
            pltpu.VMEM((CH, KEPT, TLEN), BF16),
            pltpu.VMEM((KEPT, 128), F32),
            pltpu.VMEM((NY, UNITS, 9, 16, 128), BF16),
            pltpu.VMEM((2, 16, WIN + 128), F32),
            pltpu.VMEM((16, WIN + 128), F32),
            pltpu.VMEM((UCH * TLEN, WIN), BF16),
            pltpu.VMEM((1, ENT), jnp.int32),
            pltpu.VMEM((1, ENT), jnp.int32),
            pltpu.VMEM((1, TAPS), F32),
            pltpu.SemaphoreType.DMA((4,)),
            pltpu.SemaphoreType.DMA((16,)),
            pltpu.SemaphoreType.DMA,
            pltpu.SemaphoreType.DMA,
            pltpu.SemaphoreType.DMA((2 * NY,)),
            pltpu.SemaphoreType.DMA((NY,)),
            pltpu.SemaphoreType.DMA((NY,)),
        ],
        compiler_params=pltpu.CompilerParams(
            collective_id=0, has_side_effects=True, vmem_limit_bytes=40 * 1024 * 1024
        ),
    )(
        in_hbm(destinations),
        in_hbm(offsets),
        live_counts,
        in_hbm(band_filter.reshape(1, TAPS)),
        in_hbm(records),
        in_hbm(templates),
    )
    return pl.pallas_call(
        finish,
        out_shape=jax.ShapeDtypeStruct((KEPT, WIN), F32),
        in_specs=[vmem] * 5,
        out_specs=hbm,
        scratch_shapes=[pltpu.VMEM((8, KEPT, 128), F32), pltpu.SemaphoreType.DMA((8,))],
        compiler_params=pltpu.CompilerParams(vmem_limit_bytes=8 * 1024 * 1024),
    )(*results)


def solution(mesh):
    in_specs = (
        P("tmpl", "tm", None),
        P(),
        P("tmpl", None, None),
        P("tmpl", "tm"),
        P("tmpl", "tm"),
        P("tmpl", "tm"),
    )
    return jax.shard_map(
        shards, mesh=mesh, in_specs=in_specs, out_specs=P("tmpl", "tm"), check_vma=False
    )
```

```python
import jax
import jax.numpy as jnp
from jax import lax
from jax.experimental import pallas as pl
from jax.experimental.pallas import tpu as pltpu
from jax.sharding import PartitionSpec as P

CH = 144
TAPS = 65
DEC = 8
RECLEN = 512
TLEN = 128
EPSILON = 1e-06

NTM = 64
NY = 4
ENT = 576
EPAD = 640
CAP = 16
WIRE = 10
UNITS = 3
UCH = 12
KEPT = 256
WIN = 1024
F32 = jnp.float32
BF16 = jnp.bfloat16
MESH = pl.DeviceIdType.MESH
FAR_FIRST = sorted(
    [(dx, dz, dc) for dx in range(4) for dz in range(8) for dc in range(2)][1:],
    key=lambda d: -(min(d[0], 4 - d[0]) + min(d[1], 8 - d[1])),
)
NT = (((1,), (1,)), ((), ()))


def iota(shape, dim):
    return lax.broadcasted_iota(jnp.int32, shape, dim)


def lane_take(x, index):
    return jnp.take_along_axis(x, index, axis=1)


def kernel(
    dest_hbm,
    offs_hbm,
    live_ref,
    band_hbm,
    rec_hbm,
    tmpl_hbm,
    acc,
    by_tmpl,
    by_time,
    rec,
    tmpl,
    taps,
    rows,
    ybuf,
    send,
    arr,
    wts,
    tsq,
    gall,
    g32,
    pw,
    hank,
    dest_ref,
    offs_ref,
    band_ref,
    rec_sem,
    tmpl_sem,
    a_send,
    a_recv,
    b_send,
    main_recv,
    halo_recv,
):
    me = lax.axis_index("tm")
    my = lax.axis_index("tmpl")

    rec_copy = pltpu.make_async_copy(rec_hbm.at[0], rec.at[pl.ds(0, ENT)], rec_sem.at[0])
    small = [
        pltpu.make_async_copy(dest_hbm, dest_ref, rec_sem.at[1]),
        pltpu.make_async_copy(offs_hbm, offs_ref, rec_sem.at[2]),
        pltpu.make_async_copy(band_hbm, band_ref, rec_sem.at[3]),
    ]
    for copy in small:
        copy.start()
    rec_copy.start()
    arr[...] = jnp.zeros(arr.shape, BF16)
    barrier = pltpu.get_barrier_semaphore()

    x, z, core = me // 16, (me // 2) % 8, me % 2
    partners = [
        ((x + dx) % 4) * 16 + ((z + dz) % 8) * 2 + (core + dc) % 2 for dx, dz, dc in FAR_FIRST
    ]
    for to in partners:
        pl.semaphore_signal(barrier, inc=1, device_id={"tm": to}, device_id_type=MESH)
    for i in range(1, NY):
        other = lax.rem(my + i, NY)
        pl.semaphore_signal(barrier, inc=1, device_id={"tmpl": other}, device_id_type=MESH)

        @pl.when(me < NTM - 1)
        def _():
            pl.semaphore_signal(
                barrier, inc=1, device_id={"tm": me + 1, "tmpl": other}, device_id_type=MESH
            )

    def tmpl_copy(b):
        part = pl.ds(pl.multiple_of(b * 16, 16), 16)
        return pltpu.make_async_copy(tmpl_hbm.at[part], tmpl.at[part], tmpl_sem.at[b])

    for b in range(16):
        tmpl_copy(b).start()

    rec[ENT:EPAD, :] = jnp.zeros((EPAD - ENT, RECLEN), F32)
    rows[...] = jnp.full(rows.shape, -1, jnp.int32)
    for copy in small:
        copy.wait()
    rows[0:1, 0:ENT] = dest_ref[...]
    rows[1:2, 0:ENT] = offs_ref[...]
    entry = iota((1, EPAD), 1)
    target = rows[0:1, :]
    label = jnp.maximum(rows[1:2, :], 0) // RECLEN
    chan = label // 16
    slot = label - chan * 16
    chan = chan + 4 * (chan // UCH)
    member = jnp.where(jnp.broadcast_to(target, (NTM, EPAD)) == iota((NTM, EPAD), 0), 1.0, 0.0)
    before = jnp.where(iota((EPAD, EPAD), 0) < iota((EPAD, EPAD), 1), 1.0, 0.0).astype(BF16)
    ahead = jnp.dot(member.astype(BF16), before, preferred_element_type=F32)
    rank = jnp.sum(ahead * member, axis=0, keepdims=True).astype(jnp.int32)
    live = entry < jnp.minimum(live_ref[0, 0], ENT)
    place = jnp.where(live, target * CAP + rank, -1)

    taps[...] = jnp.zeros(taps.shape, F32)
    taps[0:1, 0:TAPS] = band_ref[...]
    line = jnp.broadcast_to(taps[0:1, :], (80, 128))
    parts = []
    for s in range(4):
        tap = iota((80, 128), 1) + 128 * s + DEC * iota((80, 128), 0) - (RECLEN - DEC)
        good = (tap >= 0) & (tap < TAPS) & (iota((80, 128), 0) < 72)
        parts.append(jnp.where(good, lane_take(line, jnp.clip(tap, 0, 127)), 0.0))
    band = jnp.concatenate(parts, axis=1)
    band_hi = band.astype(BF16)
    band_lo = (band - band_hi.astype(F32)).astype(BF16)

    rec_copy.wait()
    data = rec[...]
    data_hi = data.astype(BF16)
    data_lo = (data - data_hi.astype(F32)).astype(BF16)
    both = jnp.concatenate([band_hi, band_lo], axis=0)
    both = lax.dot_general(both, data_hi, NT, preferred_element_type=F32)
    parts = lax.dot_general(band_hi, data_lo, NT, preferred_element_type=F32)
    parts += both[0:80] + both[80:160]
    row = iota((80, EPAD), 0)
    parts = jnp.where(row == 72, jnp.broadcast_to(chan.astype(F32), (80, EPAD)), parts)
    parts = jnp.where(row == 73, jnp.broadcast_to(slot.astype(F32), (80, EPAD)), parts)
    parts = jnp.concatenate([parts, jnp.zeros((48, EPAD), F32)], axis=0).astype(BF16)

    ybuf[NTM * CAP :, :] = jnp.zeros((CAP, 128), F32)
    for q in range(4):
        pick = jnp.where(
            jnp.broadcast_to(place, (256, EPAD)) == iota((256, EPAD), 0) + 256 * q, 1.0, 0.0
        ).astype(BF16)
        ybuf[256 * q : 256 * q + 256, :] = lax.dot_general(
            pick, parts, NT, preferred_element_type=F32
        )
    lane = iota((256, 128), 1)
    for q in range(4):
        own = ybuf[256 * q : 256 * q + 256, :]
        after = ybuf[256 * q + CAP : 256 * q + 256 + CAP, :]
        both = jnp.where((lane >= 80) & (lane < 90), pltpu.roll(after, 16, 1), own)
        send[16 * q : 16 * q + 16] = both.astype(BF16).reshape(16, CAP, 128)

    pl.semaphore_wait(barrier, 66 + jnp.where(me > 0, 3, 0))

    def block_copy(to, frm):
        return pltpu.make_async_remote_copy(
            src_ref=send.at[to, pl.ds(0, WIRE)],
            dst_ref=arr.at[frm, pl.ds(0, WIRE)],
            send_sem=a_send,
            recv_sem=a_recv,
            device_id={"tm": to},
            device_id_type=MESH,
        )

    for to in partners:
        block_copy(to, me).start()
    arr[me] = send[me]

    def order_templates(b, _):
        tmpl_copy(b).wait()
        part = pl.ds(pl.multiple_of(b * 16, 16), 16)
        total = jnp.zeros((16, 16, 128), F32)
        for g in range(9):
            x = tmpl[part, 16 * g : 16 * g + 16, :]
            wts[16 * g : 16 * g + 16, part, :] = jnp.transpose(x, (1, 0, 2))
            wide = x.astype(F32)
            total = total + wide * wide
        tsq[part, :] = jnp.sum(total, axis=1)
        return 0

    lax.fori_loop(0, 16, order_templates, 0)
    mean = jnp.sum(tsq[...], axis=1, keepdims=True) * (1.0 / (CH * TLEN))
    by_tmpl[...] = jnp.broadcast_to(
        1.0 / (CH * TLEN * jnp.sqrt(mean + EPSILON)), (KEPT, 128)
    )

    def all_blocks():
        return pltpu.make_async_remote_copy(
            src_ref=send.at[pl.ds(0, NTM - 1), pl.ds(0, WIRE)],
            dst_ref=arr.at[pl.ds(0, NTM - 1), pl.ds(0, WIRE)],
            send_sem=a_send,
            recv_sem=a_recv,
            device_id={"tm": me},
            device_id_type=MESH,
        )

    all_blocks().wait_recv()

    came = arr[...].reshape(NTM * CAP, 128)
    sel_row = iota((8, 128), 0)
    sel_lane = iota((8, 128), 1)
    selector = (
        ((sel_row == 0) & (sel_lane == 72))
        | ((sel_row == 1) & (sel_lane == 73))
        | ((sel_row == 2) & (sel_lane == 88))
        | ((sel_row == 3) & (sel_lane == 89))
    )
    names = lax.dot_general(
        jnp.where(selector, 1.0, 0.0).astype(BF16), came, NT, preferred_element_type=F32
    ).astype(jnp.int32)
    spot = names[0:1, :] + 48 * (15 - names[1:2, :])
    spot_next = jnp.where(names[3:4, :] == 0, names[2:3, :], -1)
    lane = iota((48, 128), 1)
    pick = jnp.where(
        jnp.broadcast_to(spot_next, (48, 1024)) == iota((48, 1024), 0), 1.0, 0.0
    ).astype(BF16)
    carry = pltpu.roll(jnp.dot(pick, came, preferred_element_type=F32), 48, 1)
    for b in range(8):
        pick = jnp.where(
            jnp.broadcast_to(spot, (96, 1024)) == iota((96, 1024), 0) + 96 * b, 1.0, 0.0
        ).astype(BF16)
        got = jnp.dot(pick, came, preferred_element_type=F32)
        odd = pltpu.roll(got[48:96], 64, 1)
        block = (
            jnp.where(lane < 72, got[0:48], 0.0)
            + jnp.where(lane >= 64, odd, 0.0)
            + jnp.where(lane < 8, carry, 0.0)
        )
        carry = odd
        gall[my, :, b + 1] = block.astype(BF16).reshape(UNITS, 16, 128)

    @pl.when(me == NTM - 1)
    def _():
        gall[:, :, 0] = jnp.zeros((NY, UNITS, 16, 128), BF16)

    def halo_copy(quarter, to_tm, to_y, k=0):
        return pltpu.make_async_remote_copy(
            src_ref=gall.at[quarter, :, 8, pl.ds(0, UCH)],
            dst_ref=gall.at[quarter, :, 0, pl.ds(0, UCH)],
            send_sem=b_send.at[4 + k],
            recv_sem=halo_recv.at[quarter],
            device_id={"tm": to_tm, "tmpl": to_y},
            device_id_type=MESH,
        )

    def main_copy(quarter, to_y, k=0):
        return pltpu.make_async_remote_copy(
            src_ref=gall.at[quarter, :, pl.ds(1, 8), pl.ds(0, UCH)],
            dst_ref=gall.at[quarter, :, pl.ds(1, 8), pl.ds(0, UCH)],
            send_sem=b_send.at[k],
            recv_sem=main_recv.at[quarter],
            device_id={"tmpl": to_y},
            device_id_type=MESH,
        )

    @pl.when(me > 0)
    def _():
        halo_copy(my, me - 1, my, 0).start()

    for i in (1, 3):
        main_copy(my, lax.rem(my + i, NY), i).start()

    @pl.when(me > 0)
    def _():
        for i in (1, 3, 2):
            halo_copy(my, me - 1, lax.rem(my + i, NY), i).start()

    def quarter_of(n):
        step = n // UNITS
        return lax.rem(my + lax.bitwise_xor(step, lax.shift_right_logical(step, 1)), NY)

    def arrive(n, mine):
        quarter = quarter_of(n)
        if not mine:
            main_copy(quarter, my).wait_recv()

        @pl.when(me < NTM - 1)
        def _():
            halo_copy(quarter, me, my).wait_recv()

    hl = iota((16, 128), 1)
    hr = iota((16, 128), 0)

    def widen(n, side, first, last):
        for b in range(first, last):
            at = slice(128 * b, 128 * b + 128)
            wide = gall[quarter_of(n), lax.rem(n, UNITS), b].astype(F32)
            wide = jnp.where(hr < UCH, wide, 0.0)
            g32[side, :, at] = wide
            pw[:, at] += wide * wide

    def expand(side, channels, first, last):
        for i in channels:
            line = [
                jnp.broadcast_to(g32[side, i : i + 1, 128 * b : 128 * b + 128], (16, 128))
                for b in range(first, last + 1)
            ]
            for s in range(8):
                from_last = hl + hr >= 128 - 16 * s
                for b in range(first, last):
                    mixed = jnp.where(from_last, line[b - first], line[b - first + 1])
                    at = i * 128 + 16 * s
                    hank[side, at : at + 16, 128 * b : 128 * b + 128] = pltpu.roll(
                        mixed, 16 * s, 1, stride=1, stride_axis=0
                    ).astype(BF16)

    def build(n, side):
        widen(n, side, 0, 9)
        expand(side, range(UCH), 0, 8)

    def correlate(n, side, lo=0, hi=WIN, channels=range(UCH)):
        c0 = quarter_of(n) * (CH // NY) + lax.rem(n, UNITS) * UCH
        left = jnp.concatenate([wts[c0 + i] for i in channels], axis=1)
        deep = slice(channels[0] * TLEN, (channels[-1] + 1) * TLEN)
        acc[:, lo:hi] += jnp.dot(left, hank[side, deep, lo:hi], preferred_element_type=F32)

    acc[...] = jnp.zeros(acc.shape, F32)
    pw[...] = jnp.zeros(pw.shape, F32)
    widen(0, 0, 1, 9)
    thirds = [range(4 * i, 4 * i + 4) for i in range(3)]
    expand(0, thirds[0], 1, 8)
    for i in range(3):
        if i < 2:
            expand(0, thirds[i + 1], 1, 8)
        correlate(0, 0, 256, WIN, thirds[i])
    arrive(0, True)
    widen(0, 0, 0, 1)
    expand(0, range(UCH), 0, 1)
    build(1, 1)
    correlate(0, 0, 0, 256)
    main_copy(my, lax.rem(my + 2, NY), 2).start()
    build(2, 0)
    correlate(1, 1)
    total_units = NY * UNITS

    def step(it, _):
        n = 2 * it

        @pl.when((it == 1) | (it == 4))
        def _():
            arrive(n + 1, False)

        build(n + 1, 1)
        correlate(n, 0)

        @pl.when(it == 2)
        def _():
            arrive(n + 2, False)

        build(n + 2, 0)
        correlate(n + 1, 1)
        return 0

    lax.fori_loop(1, total_units // 2 - 1, step, 0)
    build(total_units - 1, 1)
    energy = jnp.broadcast_to(jnp.sum(pw[...], axis=0, keepdims=True), (8, WIN + 128))
    for k in (1, 2, 4, 8, 16, 32, 64):
        energy = energy + pltpu.roll(energy, k, 1)
    by_time[...] = 1.0 / jnp.sqrt(energy[:, 128:] * (1.0 / (CH * TLEN)) + EPSILON)
    correlate(total_units - 2, 0)
    correlate(total_units - 1, 1)

    all_blocks().wait_send()
    for i in range(1, NY):
        main_copy(my, lax.rem(my + i, NY), i).wait_send()

    @pl.when(me > 0)
    def _():
        for i in range(NY):
            halo_copy(my, me - 1, lax.rem(my + i, NY), i).wait_send()


def finish(acc, by_tmpl, by_time, out_hbm, stage, sem):
    back = 127 - iota((KEPT, 128), 1)
    copies = []
    for b in range(8):
        at = pl.ds(128 * (7 - b), 128)
        part = acc[:, 128 * b : 128 * b + 128] * by_tmpl[...]
        part = part * by_time[0:1, 128 * b : 128 * b + 128]
        stage[b] = lane_take(part, back)
        copies.append(pltpu.make_async_copy(stage.at[b], out_hbm.at[:, at], sem.at[b]))
        copies[-1].start()
    for copy in copies:
        copy.wait()


def in_hbm(x):
    return pltpu.with_memory_space_constraint(x, pltpu.HBM)


def shards(records, band_filter, templates, destinations, offsets, live_counts):
    vmem = pl.BlockSpec(memory_space=pltpu.VMEM)
    hbm = pl.BlockSpec(memory_space=pltpu.HBM)
    acc, by_tmpl, by_time = pl.pallas_call(
        kernel,
        out_shape=[
            jax.ShapeDtypeStruct((KEPT, WIN), F32),
            jax.ShapeDtypeStruct((KEPT, 128), F32),
            jax.ShapeDtypeStruct((8, WIN), F32),
        ],
        in_specs=[hbm, hbm, pl.BlockSpec(memory_space=pltpu.SMEM), hbm, hbm, hbm],
        out_specs=[vmem] * 3,
        scratch_shapes=[
            pltpu.VMEM((EPAD, RECLEN), F32),
            pltpu.VMEM((KEPT, CH, TLEN), BF16),
            pltpu.VMEM((8, 128), F32),
            pltpu.VMEM((8, EPAD), jnp.int32),
            pltpu.VMEM((NTM * CAP + CAP, 128), F32),
            pltpu.VMEM((NTM, CAP, 128), BF16),
            pltpu.VMEM((NTM, CAP, 128), BF16),
            pltpu.VMEM((CH, KEPT, TLEN), BF16),
            pltpu.VMEM((KEPT, 128), F32),
            pltpu.VMEM((NY, UNITS, 9, 16, 128), BF16),
            pltpu.VMEM((2, 16, WIN + 128), F32),
            pltpu.VMEM((16, WIN + 128), F32),
            pltpu.VMEM((2, UCH * TLEN, WIN), BF16),
            pltpu.VMEM((1, ENT), jnp.int32),
            pltpu.VMEM((1, ENT), jnp.int32),
            pltpu.VMEM((1, TAPS), F32),
            pltpu.SemaphoreType.DMA((4,)),
            pltpu.SemaphoreType.DMA((16,)),
            pltpu.SemaphoreType.DMA,
            pltpu.SemaphoreType.DMA,
            pltpu.SemaphoreType.DMA((2 * NY,)),
            pltpu.SemaphoreType.DMA((NY,)),
            pltpu.SemaphoreType.DMA((NY,)),
        ],
        compiler_params=pltpu.CompilerParams(
            collective_id=0, has_side_effects=True, vmem_limit_bytes=52 * 1024 * 1024
        ),
    )(
        in_hbm(destinations),
        in_hbm(offsets),
        live_counts,
        in_hbm(band_filter.reshape(1, TAPS)),
        in_hbm(records),
        in_hbm(templates),
    )
    return pl.pallas_call(
        finish,
        out_shape=jax.ShapeDtypeStruct((KEPT, WIN), F32),
        in_specs=[vmem] * 3,
        out_specs=hbm,
        scratch_shapes=[pltpu.VMEM((8, KEPT, 128), F32), pltpu.SemaphoreType.DMA((8,))],
        compiler_params=pltpu.CompilerParams(vmem_limit_bytes=8 * 1024 * 1024),
    )(acc, by_tmpl, by_time)


def solution(mesh):
    in_specs = (
        P("tmpl", "tm", None),
        P(),
        P("tmpl", None, None),
        P("tmpl", "tm"),
        P("tmpl", "tm"),
        P("tmpl", "tm"),
    )
    return jax.shard_map(
        shards, mesh=mesh, in_specs=in_specs, out_specs=P("tmpl", "tm"), check_vma=False
    )
```

```python
import jax
import jax.numpy as jnp
from jax import lax
from jax.experimental import pallas as pl
from jax.experimental.pallas import tpu as pltpu
from jax.sharding import PartitionSpec as P

CH = 144
TAPS = 65
DEC = 8
RECLEN = 512
TLEN = 128
EPSILON = 1e-06

NTM = 64
NY = 4
ENT = 576
EPAD = 640
CAP = 16
WIRE = 10
UNITS = 3
UCH = 12
KEPT = 256
WIN = 1024
F32 = jnp.float32
BF16 = jnp.bfloat16
MESH = pl.DeviceIdType.MESH
FAR_FIRST = sorted(
    [(dx, dz, dc) for dx in range(4) for dz in range(8) for dc in range(2)][1:],
    key=lambda d: -(min(d[0], 4 - d[0]) + min(d[1], 8 - d[1])),
)
NT = (((1,), (1,)), ((), ()))


def iota(shape, dim):
    return lax.broadcasted_iota(jnp.int32, shape, dim)


def lane_take(x, index):
    return jnp.take_along_axis(x, index, axis=1)


def kernel(
    dest_hbm,
    offs_hbm,
    live_ref,
    band_hbm,
    rec_hbm,
    tmpl_hbm,
    acc,
    by_tmpl,
    by_time,
    rec,
    tmpl,
    taps,
    rows,
    ybuf,
    send,
    arr,
    wts,
    tsq,
    gall,
    g32,
    pw,
    hank,
    dest_ref,
    offs_ref,
    band_ref,
    rec_sem,
    tmpl_sem,
    a_send,
    a_recv,
    b_send,
    main_recv,
    halo_recv,
):
    me = lax.axis_index("tm")
    my = lax.axis_index("tmpl")

    pieces = [
        pltpu.make_async_copy(
            rec_hbm.at[0, pl.ds(144 * i, 144)], rec.at[pl.ds(144 * i, 144)], rec_sem.at[4 + i]
        )
        for i in range(4)
    ]
    small = [
        pltpu.make_async_copy(dest_hbm, dest_ref, rec_sem.at[1]),
        pltpu.make_async_copy(offs_hbm, offs_ref, rec_sem.at[2]),
        pltpu.make_async_copy(band_hbm, band_ref, rec_sem.at[3]),
    ]
    for copy in small:
        copy.start()
    for copy in pieces:
        copy.start()
    arr[...] = jnp.zeros(arr.shape, BF16)
    barrier = pltpu.get_barrier_semaphore()

    x, z, core = me // 16, (me // 2) % 8, me % 2
    partners = [
        ((x + dx) % 4) * 16 + ((z + dz) % 8) * 2 + (core + dc) % 2 for dx, dz, dc in FAR_FIRST
    ]
    for to in partners:
        pl.semaphore_signal(barrier, inc=1, device_id={"tm": to}, device_id_type=MESH)
    for i in range(1, NY):
        other = lax.rem(my + i, NY)
        pl.semaphore_signal(barrier, inc=1, device_id={"tmpl": other}, device_id_type=MESH)

        @pl.when(me < NTM - 1)
        def _():
            pl.semaphore_signal(
                barrier, inc=1, device_id={"tm": me + 1, "tmpl": other}, device_id_type=MESH
            )

    def tmpl_copy(b):
        part = pl.ds(pl.multiple_of(b * 16, 16), 16)
        return pltpu.make_async_copy(tmpl_hbm.at[part], tmpl.at[part], tmpl_sem.at[b])

    rec[ENT:EPAD, :] = jnp.zeros((EPAD - ENT, RECLEN), F32)
    rows[...] = jnp.full(rows.shape, -1, jnp.int32)
    for copy in small:
        copy.wait()
    rows[0:1, 0:ENT] = dest_ref[...]
    rows[1:2, 0:ENT] = offs_ref[...]
    entry = iota((1, EPAD), 1)
    target = rows[0:1, :]
    label = jnp.maximum(rows[1:2, :], 0) // RECLEN
    chan = label // 16
    slot = label - chan * 16
    chan = chan + 4 * (chan // UCH)
    member = jnp.where(jnp.broadcast_to(target, (NTM, EPAD)) == iota((NTM, EPAD), 0), 1.0, 0.0)
    before = jnp.where(iota((EPAD, EPAD), 0) < iota((EPAD, EPAD), 1), 1.0, 0.0).astype(BF16)
    ahead = jnp.dot(member.astype(BF16), before, preferred_element_type=F32)
    rank = jnp.sum(ahead * member, axis=0, keepdims=True).astype(jnp.int32)
    live = entry < jnp.minimum(live_ref[0, 0], ENT)
    place = jnp.where(live, target * CAP + rank, -1)

    taps[...] = jnp.zeros(taps.shape, F32)
    taps[0:1, 0:TAPS] = band_ref[...]
    line = jnp.broadcast_to(taps[0:1, :], (80, 128))
    parts = []
    for s in range(4):
        tap = iota((80, 128), 1) + 128 * s + DEC * iota((80, 128), 0) - (RECLEN - DEC)
        good = (tap >= 0) & (tap < TAPS) & (iota((80, 128), 0) < 72)
        parts.append(jnp.where(good, lane_take(line, jnp.clip(tap, 0, 127)), 0.0))
    band = jnp.concatenate(parts, axis=1)
    band_hi = band.astype(BF16)
    band_lo = (band - band_hi.astype(F32)).astype(BF16)

    for copy in pieces:
        copy.wait()
    for b in range(16):
        tmpl_copy(b).start()
    data = rec[...]
    data_hi = data.astype(BF16)
    data_lo = (data - data_hi.astype(F32)).astype(BF16)
    both = jnp.concatenate([band_hi, band_lo], axis=0)
    both = lax.dot_general(both, data_hi, NT, preferred_element_type=F32)
    parts = lax.dot_general(band_hi, data_lo, NT, preferred_element_type=F32)
    parts += both[0:80] + both[80:160]
    row = iota((80, EPAD), 0)
    parts = jnp.where(row == 72, jnp.broadcast_to(chan.astype(F32), (80, EPAD)), parts)
    parts = jnp.where(row == 73, jnp.broadcast_to(slot.astype(F32), (80, EPAD)), parts)
    parts = jnp.concatenate([parts, jnp.zeros((48, EPAD), F32)], axis=0).astype(BF16)

    ybuf[NTM * CAP :, :] = jnp.zeros((CAP, 128), F32)
    for q in range(4):
        pick = jnp.where(
            jnp.broadcast_to(place, (256, EPAD)) == iota((256, EPAD), 0) + 256 * q, 1.0, 0.0
        ).astype(BF16)
        ybuf[256 * q : 256 * q + 256, :] = lax.dot_general(
            pick, parts, NT, preferred_element_type=F32
        )
    lane = iota((256, 128), 1)
    for q in range(4):
        own = ybuf[256 * q : 256 * q + 256, :]
        after = ybuf[256 * q + CAP : 256 * q + 256 + CAP, :]
        both = jnp.where((lane >= 80) & (lane < 90), pltpu.roll(after, 16, 1), own)
        send[16 * q : 16 * q + 16] = both.astype(BF16).reshape(16, CAP, 128)

    pl.semaphore_wait(barrier, 66 + jnp.where(me > 0, 3, 0))

    def block_copy(to, frm):
        return pltpu.make_async_remote_copy(
            src_ref=send.at[to, pl.ds(0, WIRE)],
            dst_ref=arr.at[frm, pl.ds(0, WIRE)],
            send_sem=a_send,
            recv_sem=a_recv,
            device_id={"tm": to},
            device_id_type=MESH,
        )

    for to in partners:
        block_copy(to, me).start()
    arr[me] = send[me]

    def order_templates(b, _):
        tmpl_copy(b).wait()
        part = pl.ds(pl.multiple_of(b * 16, 16), 16)
        total = jnp.zeros((16, 16, 128), F32)
        for g in range(9):
            x = tmpl[part, 16 * g : 16 * g + 16, :]
            wts[16 * g : 16 * g + 16, part, :] = jnp.transpose(x, (1, 0, 2))
            wide = x.astype(F32)
            total = total + wide * wide
        tsq[part, :] = jnp.sum(total, axis=1)
        return 0

    lax.fori_loop(0, 16, order_templates, 0)
    mean = jnp.sum(tsq[...], axis=1, keepdims=True) * (1.0 / (CH * TLEN))
    by_tmpl[...] = jnp.broadcast_to(
        1.0 / (CH * TLEN * jnp.sqrt(mean + EPSILON)), (KEPT, 128)
    )

    def all_blocks():
        return pltpu.make_async_remote_copy(
            src_ref=send.at[pl.ds(0, NTM - 1), pl.ds(0, WIRE)],
            dst_ref=arr.at[pl.ds(0, NTM - 1), pl.ds(0, WIRE)],
            send_sem=a_send,
            recv_sem=a_recv,
            device_id={"tm": me},
            device_id_type=MESH,
        )

    all_blocks().wait_recv()

    came = arr[...].reshape(NTM * CAP, 128)
    sel_row = iota((8, 128), 0)
    sel_lane = iota((8, 128), 1)
    selector = (
        ((sel_row == 0) & (sel_lane == 72))
        | ((sel_row == 1) & (sel_lane == 73))
        | ((sel_row == 2) & (sel_lane == 88))
        | ((sel_row == 3) & (sel_lane == 89))
    )
    names = lax.dot_general(
        jnp.where(selector, 1.0, 0.0).astype(BF16), came, NT, preferred_element_type=F32
    ).astype(jnp.int32)
    spot = names[0:1, :] + 48 * (15 - names[1:2, :])
    spot_next = jnp.where(names[3:4, :] == 0, names[2:3, :], -1)
    lane = iota((48, 128), 1)
    pick = jnp.where(
        jnp.broadcast_to(spot_next, (48, 1024)) == iota((48, 1024), 0), 1.0, 0.0
    ).astype(BF16)
    carry = pltpu.roll(jnp.dot(pick, came, preferred_element_type=F32), 48, 1)
    for b in range(8):
        pick = jnp.where(
            jnp.broadcast_to(spot, (96, 1024)) == iota((96, 1024), 0) + 96 * b, 1.0, 0.0
        ).astype(BF16)
        got = jnp.dot(pick, came, preferred_element_type=F32)
        odd = pltpu.roll(got[48:96], 64, 1)
        block = (
            jnp.where(lane < 72, got[0:48], 0.0)
            + jnp.where(lane >= 64, odd, 0.0)
            + jnp.where(lane < 8, carry, 0.0)
        )
        carry = odd
        gall[my, :, b + 1] = block.astype(BF16).reshape(UNITS, 16, 128)

    @pl.when(me == NTM - 1)
    def _():
        gall[:, :, 0] = jnp.zeros((NY, UNITS, 16, 128), BF16)

    def halo_copy(quarter, to_tm, to_y, k=0):
        return pltpu.make_async_remote_copy(
            src_ref=gall.at[quarter, :, 8, pl.ds(0, UCH)],
            dst_ref=gall.at[quarter, :, 0, pl.ds(0, UCH)],
            send_sem=b_send.at[4 + k],
            recv_sem=halo_recv.at[quarter],
            device_id={"tm": to_tm, "tmpl": to_y},
            device_id_type=MESH,
        )

    def main_copy(quarter, to_y, k=0):
        return pltpu.make_async_remote_copy(
            src_ref=gall.at[quarter, :, pl.ds(1, 8), pl.ds(0, UCH)],
            dst_ref=gall.at[quarter, :, pl.ds(1, 8), pl.ds(0, UCH)],
            send_sem=b_send.at[k],
            recv_sem=main_recv.at[quarter],
            device_id={"tmpl": to_y},
            device_id_type=MESH,
        )

    @pl.when(me > 0)
    def _():
        halo_copy(my, me - 1, my, 0).start()

    for i in (1, 3):
        main_copy(my, lax.rem(my + i, NY), i).start()

    @pl.when(me > 0)
    def _():
        for i in (1, 3, 2):
            halo_copy(my, me - 1, lax.rem(my + i, NY), i).start()

    def quarter_of(n):
        step = n // UNITS
        return lax.rem(my + lax.bitwise_xor(step, lax.shift_right_logical(step, 1)), NY)

    def arrive(n, mine):
        quarter = quarter_of(n)
        if not mine:
            main_copy(quarter, my).wait_recv()

        @pl.when(me < NTM - 1)
        def _():
            halo_copy(quarter, me, my).wait_recv()

    hl = iota((16, 128), 1)
    hr = iota((16, 128), 0)

    def widen(n, side, first, last):
        for b in range(first, last):
            at = slice(128 * b, 128 * b + 128)
            wide = gall[quarter_of(n), lax.rem(n, UNITS), b].astype(F32)
            wide = jnp.where(hr < UCH, wide, 0.0)
            g32[side, :, at] = wide
            pw[:, at] += wide * wide

    def expand(side, channels, first, last):
        for i in channels:
            line = [
                jnp.broadcast_to(g32[side, i : i + 1, 128 * b : 128 * b + 128], (16, 128))
                for b in range(first, last + 1)
            ]
            for s in range(8):
                from_last = hl + hr >= 128 - 16 * s
                for b in range(first, last):
                    mixed = jnp.where(from_last, line[b - first], line[b - first + 1])
                    at = i * 128 + 16 * s
                    hank[side, at : at + 16, 128 * b : 128 * b + 128] = pltpu.roll(
                        mixed, 16 * s, 1, stride=1, stride_axis=0
                    ).astype(BF16)

    def build(n, side):
        widen(n, side, 0, 9)
        expand(side, range(UCH), 0, 8)

    def correlate(n, side, lo=0, hi=WIN, channels=range(UCH)):
        c0 = quarter_of(n) * (CH // NY) + lax.rem(n, UNITS) * UCH
        left = jnp.concatenate([wts[c0 + i] for i in channels], axis=1)
        deep = slice(channels[0] * TLEN, (channels[-1] + 1) * TLEN)
        acc[:, lo:hi] += jnp.dot(left, hank[side, deep, lo:hi], preferred_element_type=F32)

    acc[...] = jnp.zeros(acc.shape, F32)
    pw[...] = jnp.zeros(pw.shape, F32)
    widen(0, 0, 1, 9)
    thirds = [range(4 * i, 4 * i + 4) for i in range(3)]
    expand(0, thirds[0], 1, 8)
    for i in range(3):
        if i < 2:
            expand(0, thirds[i + 1], 1, 8)
        correlate(0, 0, 256, WIN, thirds[i])
    arrive(0, True)
    widen(0, 0, 0, 1)
    expand(0, range(UCH), 0, 1)
    build(1, 1)
    correlate(0, 0, 0, 256)
    main_copy(my, lax.rem(my + 2, NY), 2).start()
    build(2, 0)
    correlate(1, 1)
    total_units = NY * UNITS

    def step(it, _):
        n = 2 * it

        @pl.when((it == 1) | (it == 4))
        def _():
            arrive(n + 1, False)

        build(n + 1, 1)
        correlate(n, 0)

        @pl.when(it == 2)
        def _():
            arrive(n + 2, False)

        build(n + 2, 0)
        correlate(n + 1, 1)
        return 0

    lax.fori_loop(1, total_units // 2 - 1, step, 0)
    build(total_units - 1, 1)
    energy = jnp.broadcast_to(jnp.sum(pw[...], axis=0, keepdims=True), (8, WIN + 128))
    for k in (1, 2, 4, 8, 16, 32, 64):
        energy = energy + pltpu.roll(energy, k, 1)
    by_time[...] = 1.0 / jnp.sqrt(energy[:, 128:] * (1.0 / (CH * TLEN)) + EPSILON)
    correlate(total_units - 2, 0)
    correlate(total_units - 1, 1)

    all_blocks().wait_send()
    for i in range(1, NY):
        main_copy(my, lax.rem(my + i, NY), i).wait_send()

    @pl.when(me > 0)
    def _():
        for i in range(NY):
            halo_copy(my, me - 1, lax.rem(my + i, NY), i).wait_send()


def finish(acc, by_tmpl, by_time, out_hbm, stage, sem):
    back = 127 - iota((KEPT, 128), 1)
    copies = []
    for b in range(8):
        at = pl.ds(128 * (7 - b), 128)
        part = acc[:, 128 * b : 128 * b + 128] * by_tmpl[...]
        part = part * by_time[0:1, 128 * b : 128 * b + 128]
        stage[b] = lane_take(part, back)
        copies.append(pltpu.make_async_copy(stage.at[b], out_hbm.at[:, at], sem.at[b]))
        copies[-1].start()
    for copy in copies:
        copy.wait()


def in_hbm(x):
    return pltpu.with_memory_space_constraint(x, pltpu.HBM)


def shards(records, band_filter, templates, destinations, offsets, live_counts):
    vmem = pl.BlockSpec(memory_space=pltpu.VMEM)
    hbm = pl.BlockSpec(memory_space=pltpu.HBM)
    acc, by_tmpl, by_time = pl.pallas_call(
        kernel,
        out_shape=[
            jax.ShapeDtypeStruct((KEPT, WIN), F32),
            jax.ShapeDtypeStruct((KEPT, 128), F32),
            jax.ShapeDtypeStruct((8, WIN), F32),
        ],
        in_specs=[hbm, hbm, pl.BlockSpec(memory_space=pltpu.SMEM), hbm, hbm, hbm],
        out_specs=[vmem] * 3,
        scratch_shapes=[
            pltpu.VMEM((EPAD, RECLEN), F32),
            pltpu.VMEM((KEPT, CH, TLEN), BF16),
            pltpu.VMEM((8, 128), F32),
            pltpu.VMEM((8, EPAD), jnp.int32),
            pltpu.VMEM((NTM * CAP + CAP, 128), F32),
            pltpu.VMEM((NTM, CAP, 128), BF16),
            pltpu.VMEM((NTM, CAP, 128), BF16),
            pltpu.VMEM((CH, KEPT, TLEN), BF16),
            pltpu.VMEM((KEPT, 128), F32),
            pltpu.VMEM((NY, UNITS, 9, 16, 128), BF16),
            pltpu.VMEM((2, 16, WIN + 128), F32),
            pltpu.VMEM((16, WIN + 128), F32),
            pltpu.VMEM((2, UCH * TLEN, WIN), BF16),
            pltpu.VMEM((1, ENT), jnp.int32),
            pltpu.VMEM((1, ENT), jnp.int32),
            pltpu.VMEM((1, TAPS), F32),
            pltpu.SemaphoreType.DMA((8,)),
            pltpu.SemaphoreType.DMA((16,)),
            pltpu.SemaphoreType.DMA,
            pltpu.SemaphoreType.DMA,
            pltpu.SemaphoreType.DMA((2 * NY,)),
            pltpu.SemaphoreType.DMA((NY,)),
            pltpu.SemaphoreType.DMA((NY,)),
        ],
        compiler_params=pltpu.CompilerParams(
            collective_id=0, has_side_effects=True, vmem_limit_bytes=52 * 1024 * 1024
        ),
    )(
        in_hbm(destinations),
        in_hbm(offsets),
        live_counts,
        in_hbm(band_filter.reshape(1, TAPS)),
        in_hbm(records),
        in_hbm(templates),
    )
    return pl.pallas_call(
        finish,
        out_shape=jax.ShapeDtypeStruct((KEPT, WIN), F32),
        in_specs=[vmem] * 3,
        out_specs=hbm,
        scratch_shapes=[pltpu.VMEM((8, KEPT, 128), F32), pltpu.SemaphoreType.DMA((8,))],
        compiler_params=pltpu.CompilerParams(vmem_limit_bytes=8 * 1024 * 1024),
    )(acc, by_tmpl, by_time)


def solution(mesh):
    in_specs = (
        P("tmpl", "tm", None),
        P(),
        P("tmpl", None, None),
        P("tmpl", "tm"),
        P("tmpl", "tm"),
        P("tmpl", "tm"),
    )
    return jax.shard_map(
        shards, mesh=mesh, in_specs=in_specs, out_specs=P("tmpl", "tm"), check_vma=False
    )
```
